256 devices in a mesh: gx: 16 (over z_hi, x), gy: 16 (over z_lo, y, core).
Axes of the slice: x: 4, y: 4, z: 8 (z_hi: 4, z_lo: 2; z = z_hi * 2 + z_lo), core: 2. Of those that a mesh axis runs over, the one named last changes fastest.
Arguments:
- moving_image: bfloat16 [16, 512, 4096], P(None, 'gx', 'gy'), may hold values from -6 to 6, as said below
- fixed_image: bfloat16 [16, 512, 4096], P(None, 'gx', 'gy'), may hold values from -6 to 6, as said below
- velocity: float32 [3, 16, 512, 4096], P(None, None, 'gx', 'gy'), may hold values from 0 to 1
- offsets: int32 [3, 32, 32], P(None, 'gx', 'gy'), may hold values from -7 to 7, as said below
- tissue: int32 [32, 32], P('gx', 'gy'), may hold values from 0 to 1, as said below
Outputs:
- update: float32 [3, 16, 512, 4096], P(None, None, 'gx', 'gy')
- similarity_loss: float32 [], replicated
The draws below stay inside these ranges and needn't reach their ends.
Inputs may be any that keep to these rules, and one draw needn't show every extreme that they name: `moving_image`: the images stay within -6 to 6. `fixed_image`: the images stay within -6 to 6. `offsets`: channel 0 lies in -2 to 2, channels 1 and 2 in -7 to 7; each end is taken by some block. 1 marks a block that holds tissue; some blocks hold tissue.
All inputs are finite; a program needn't handle non-finite values.
Results may differ from the reference program's by a relative error of at most 0.0011.
Values may be sent and summed in bfloat16 or wider, within the bound.
No kernel may reach another device: no remote copies, remote signals or barrier semaphores. Data moves between devices by JAX's collectives and lax.ppermute only.
A program may use at most 64 MiB of HBM per device.

```python
import math
import jax
import jax.numpy as jnp
from jax import lax

DEPTH = 16
BX = 16
BY = 128
REACH = 7
ZREACH = 2
NX = 512
NY = 4096


def base_pattern(key):
    pattern_key = jax.random.fold_in(key, 101)
    subkeys = jax.random.split(pattern_key, 5)
    wave_x = jax.random.randint(subkeys[0], (6,), -4, 5)
    wave_y = jax.random.randint(subkeys[1], (6,), -4, 5)
    wave_z = jax.random.randint(subkeys[2], (6,), -2, 3)
    phases = jax.random.uniform(subkeys[3], (6,), minval=0.0, maxval=2.0 * math.pi)
    amplitude = jax.random.uniform(subkeys[4], (6,), minval=0.3, maxval=0.6)
    index_z = jnp.arange(DEPTH, dtype=jnp.int32)[:, None, None]
    index_x = jnp.arange(NX, dtype=jnp.int32)[None, :, None]
    index_y = jnp.arange(NY, dtype=jnp.int32)[None, None, :]
    pattern = jnp.zeros((DEPTH, NX, NY), jnp.float32)
    for wave in range(6):
        cycle = (wave_x[wave] * index_x + wave_y[wave] * index_y) % 256
        vertical = wave_z[wave] * index_z % 32
        angle = 2.0 * math.pi / 256.0 * cycle.astype(jnp.float32) + 2.0 * math.pi / 32.0 * vertical.astype(jnp.float32) + phases[wave]
        pattern = pattern + amplitude[wave] * jnp.sin(angle)
    return pattern


def image_noise(key, salt):
    noise_key = jax.random.fold_in(key, salt)
    return 0.6 * jnp.clip(jax.random.normal(noise_key, (DEPTH, NX, NY), jnp.float32), -4.0, 4.0)


def draw_moving_image(key, part):
    return (base_pattern(key) + image_noise(key, 303)).astype(jnp.bfloat16)


def draw_fixed_image(key, part):
    return (base_pattern(key) + image_noise(key, 202)).astype(jnp.bfloat16)


def draw_offsets(key, part):
    block_rows = NX // BX
    block_cols = NY // BY
    subkeys = jax.random.split(jax.random.fold_in(key, 404), 4)
    vertical = jax.random.randint(subkeys[0], (1, block_rows, block_cols), -ZREACH, ZREACH + 1)
    planar = jax.random.randint(subkeys[1], (2, block_rows, block_cols), -REACH, REACH + 1)
    shifts = jnp.concatenate([vertical, planar], axis=0)
    total_blocks = block_rows * block_cols
    flat_index = jnp.arange(total_blocks, dtype=jnp.int32).reshape(block_rows, block_cols)
    high_pick = jax.random.randint(subkeys[2], (), 0, total_blocks)
    low_pick = (high_pick + 1 + jax.random.randint(subkeys[3], (), 0, total_blocks - 1)) % total_blocks
    reach_bound = jnp.array([ZREACH, REACH, REACH], jnp.int32)[:, None, None]
    shifts = jnp.where((flat_index == high_pick)[None], reach_bound, shifts)
    shifts = jnp.where((flat_index == low_pick)[None], -reach_bound, shifts)
    return shifts.astype(jnp.int32)


def draw_tissue(key, part):
    block_rows = NX // BX
    block_cols = NY // BY
    draw_level = jax.random.randint(jax.random.fold_in(key, 505), (block_rows, block_cols), 0, block_rows)
    row_index = jnp.arange(block_rows, dtype=jnp.int32)[:, None]
    return (draw_level < row_index + block_rows // 4).astype(jnp.int32)


def level_of(stream_key, shape, shards, smallest, top_value):
    def one(position, blocks):
        draws = jax.random.uniform(jax.random.fold_in(jax.random.fold_in(stream_key, 6), position), (blocks,), jnp.float32, smallest / len(shards), top_value / len(shards))
        return jnp.repeat(jnp.exp(draws), shape[position] // blocks).reshape((-1,) + (1,) * (len(shape) - position - 1))

    gain = one(*shards[0])
    for cut in shards[1:]:
        gain = gain * one(*cut)
    return gain


def setup_inputs(seed: int = 0) -> dict:
    keys = jax.random.split(jax.random.key(seed), 6)
    return {
        "moving_image": draw_moving_image(jax.random.fold_in(keys[5], 71), 0),
        "fixed_image": draw_fixed_image(jax.random.fold_in(keys[5], 71), 0),
        "velocity": jnp.clip(1.0 * jax.random.uniform(keys[2], (3, DEPTH, NX, NY), jnp.float32) ** level_of(keys[2], (3, DEPTH, NX, NY), ((2, 16), (3, 16)), -0.2, 0.2), 0.0, 1.0),
        "offsets": draw_offsets(jax.random.fold_in(keys[5], 71), 0),
        "tissue": draw_tissue(jax.random.fold_in(keys[5], 71), 0),
    }


BOX_RADIUS = 4
GAUSS_RADIUS = 7
GAUSS_SIGMA = 3.0
WINDOW_COUNT = 729.0
VAR_EPSILON = 1e-5
STEP_RATE = 16.0


def gauss_weights():
    raw_weights = [math.exp(-float(tap * tap) / (2.0 * GAUSS_SIGMA * GAUSS_SIGMA)) for tap in range(-GAUSS_RADIUS, GAUSS_RADIUS + 1)]
    weight_total = sum(raw_weights)
    return [weight_value / weight_total for weight_value in raw_weights]


def box_weights():
    return [1.0] * (2 * BOX_RADIUS + 1)


def filter_valid(volume, weights, dim_index):
    length = volume.shape[dim_index] - (len(weights) - 1)
    summed = weights[0] * lax.slice_in_dim(volume, 0, length, axis=dim_index)
    for tap_index in range(1, len(weights)):
        summed = summed + weights[tap_index] * lax.slice_in_dim(volume, tap_index, tap_index + length, axis=dim_index)
    return summed


def filter_padded(volume, weights, dim_index):
    radius = (len(weights) - 1) // 2
    widths = [(0, 0)] * volume.ndim
    widths[dim_index] = (radius, radius)
    return filter_valid(jnp.pad(volume, widths), weights, dim_index)


def interpolate(sampler, fraction):
    weights_z = (1.0 - fraction[0], fraction[0])
    weights_x = (1.0 - fraction[1], fraction[1])
    weights_y = (1.0 - fraction[2], fraction[2])
    slope_signs = (-1.0, 1.0)
    results = None
    for corner_z in (0, 1):
        for corner_x in (0, 1):
            for corner_y in (0, 1):
                sample = sampler(corner_z, corner_x, corner_y)
                planar = weights_x[corner_x] * weights_y[corner_y]
                terms = (weights_z[corner_z] * planar * sample,
                         slope_signs[corner_z] * planar * sample,
                         weights_z[corner_z] * slope_signs[corner_x] * weights_y[corner_y] * sample,
                         weights_z[corner_z] * weights_x[corner_x] * slope_signs[corner_y] * sample)
                if results is None:
                    results = terms
                else:
                    results = tuple(results[item] + terms[item] for item in range(4))
    return results


def window_terms(image_sum, target_sum, image_square, target_square, product_sum, tissue_mask):
    cross_sum = product_sum - image_sum * target_sum / WINDOW_COUNT
    image_var = image_square - image_sum * image_sum / WINDOW_COUNT
    target_var = target_square - target_sum * target_sum / WINDOW_COUNT
    denominator = image_var * target_var + VAR_EPSILON
    ncc_value = cross_sum * cross_sum / denominator
    quotient = cross_sum / denominator
    second = quotient * quotient * target_var
    adjoint_sum = (2.0 / WINDOW_COUNT) * tissue_mask * (quotient * target_sum - second * image_sum)
    adjoint_square = tissue_mask * second
    adjoint_product = -2.0 * tissue_mask * quotient
    return ncc_value, adjoint_sum, adjoint_square, adjoint_product


def box_full(volume):
    weights = box_weights()
    return filter_padded(filter_padded(filter_padded(volume, weights, 0), weights, 1), weights, 2)


def reference(moving_image, fixed_image, velocity, offsets, tissue):
    slab_depth, extent_x, extent_y = moving_image.shape
    depth_pad = ZREACH + 1
    plane_pad = REACH + 1
    padded = jnp.pad(moving_image, ((depth_pad, depth_pad), (plane_pad, plane_pad), (plane_pad, plane_pad)))
    voxel_offsets = jnp.repeat(jnp.repeat(offsets, BX, axis=1), BY, axis=2).astype(jnp.int32)
    index_z = jnp.arange(slab_depth, dtype=jnp.int32)[:, None, None] + voxel_offsets[0][None] + depth_pad
    index_x = (jnp.arange(extent_x, dtype=jnp.int32)[:, None] + voxel_offsets[1] + plane_pad)[None]
    index_y = (jnp.arange(extent_y, dtype=jnp.int32)[None, :] + voxel_offsets[2] + plane_pad)[None]

    def sampler(corner_z, corner_x, corner_y):
        return padded[index_z + corner_z, index_x + corner_x, index_y + corner_y].astype(jnp.float32)

    warped, slope_z, slope_x, slope_y = interpolate(sampler, velocity)
    warped_low = warped.astype(jnp.bfloat16)
    image_value = lax.optimization_barrier(warped_low).astype(jnp.float32)
    target_value = fixed_image.astype(jnp.float32)
    tissue_mask = jnp.repeat(jnp.repeat(tissue, BX, axis=0), BY, axis=1).astype(jnp.float32)[None]
    ncc_value, adjoint_sum, adjoint_square, adjoint_product = window_terms(
        box_full(image_value), box_full(target_value), box_full(image_value * image_value),
        box_full(target_value * target_value), box_full(image_value * target_value), tissue_mask)
    grad_image = box_full(adjoint_sum) + 2.0 * image_value * box_full(adjoint_square) + target_value * box_full(adjoint_product)
    gradient = jnp.stack([grad_image * slope_z, grad_image * slope_x, grad_image * slope_y])
    gauss = gauss_weights()
    smoothed = filter_padded(filter_padded(filter_padded(gradient, gauss, 2), gauss, 3), gauss, 1)
    update = -STEP_RATE * smoothed
    tissue_total = jnp.sum(tissue).astype(jnp.float32)
    similarity_loss = -jnp.sum(tissue_mask * ncc_value) / (tissue_total * float(BX * BY * DEPTH))
    return update, similarity_loss
```

```python
import functools
import math

import jax
import jax.numpy as jnp
import numpy as np
from jax import lax
from jax.experimental import pallas as pl
from jax.experimental.pallas import tpu as pltpu
from jax.sharding import PartitionSpec as P

DEPTH = 16
BX = 16
BY = 128
ROWS = 32
EXT = 48
OUT = 40
LANES = 128
GAUSS_RADIUS = 7
GAUSS_SIGMA = 3.0
WINDOW_COUNT = 729.0
VAR_EPSILON = 1e-05
STEP_RATE = 16.0
F32 = jnp.float32
BF16 = jnp.bfloat16

VMEM_SPEC = pl.BlockSpec(memory_space=pltpu.VMEM)
SMEM_SPEC = pl.BlockSpec(memory_space=pltpu.SMEM)
ANY_SPEC = pl.BlockSpec(memory_space=pl.ANY)

PX, PY, HAS_L, HAS_R, OFF, TIS = 0, 1, 2, 3, 4, 16


def gauss_weights():
    raw = [
        math.exp(-float(tap * tap) / (2.0 * GAUSS_SIGMA * GAUSS_SIGMA))
        for tap in range(-GAUSS_RADIUS, GAUSS_RADIUS + 1)
    ]
    total = sum(raw)
    return [w / total for w in raw]


def lane_iota(shape):
    return lax.broadcasted_iota(jnp.int32, shape, len(shape) - 1)


def roll(x, shift):
    shift = shift % LANES
    return x if shift == 0 else pltpu.roll(x, shift, len(x.shape) - 1)


def pack_edge(tile, groups, last):
    rows = tile.shape[0] // groups
    width = LANES // groups
    lane = lane_iota((rows, LANES))
    acc = None
    for k in range(groups):
        piece = roll(tile[k * rows : (k + 1) * rows], width * (k + 1) if last else width * k)
        acc = piece if acc is None else jnp.where(lane // width == k, piece, acc)
    return acc


def unpack_group(right, left, k, groups):
    width = LANES // groups
    r = roll(right, -width * k)
    l = roll(left, -width * (k + 1))
    return jnp.where(lane_iota(r.shape) < LANES // 2, r, l)


def pick(flag, a, b):
    return jnp.where(flag == 0, a, b)


def planes(x, rows):
    return x.reshape(DEPTH, rows, x.shape[-1])


def edge_x_kernel(s_ref, m_ref, f_ref, e_ref, o_ref):
    px = s_ref[PX]
    lane = lane_iota((16, 2 * LANES))
    for n, ref in enumerate((m_ref, f_ref)):
        v = planes(ref[...].astype(F32), ROWS)
        first = v[:, :8].reshape(128, 2 * LANES)
        last = v[:, 24:].reshape(128, 2 * LANES)
        e_ref[128 * n : 128 * n + 128] = pick(px, last, first).astype(BF16)
        o_ref[128 * n : 128 * n + 128] = pick(px, first, last).astype(BF16)
    t = [[s_ref[TIS + 2 * i + j].astype(F32) for j in range(2)] for i in range(2)]
    first = jnp.where(lane < LANES, t[0][0], t[0][1])
    last = jnp.where(lane < LANES, t[1][0], t[1][1])
    e_ref[256:272] = pick(px, last, first).astype(BF16)
    o_ref[256:272] = pick(px, first, last).astype(BF16)


def edge_v_kernel(s_ref, v_ref, e_ref, o_ref):
    py = s_ref[PY]
    for c in range(3):
        first = pack_edge(v_ref[c, :, :LANES], 8, False)
        last = pack_edge(v_ref[c, :, LANES:], 8, True)
        for ref, val in ((e_ref, pick(py, last, first)), (o_ref, pick(py, first, last))):
            hi = val.astype(BF16)
            ref[128 * c : 128 * c + 64] = hi
            ref[128 * c + 64 : 128 * c + 128] = (val - hi.astype(F32)).astype(BF16)


def before_after(px, e, o):
    return pick(px, o, e), pick(px, e, o)


def extended(own, e_ref, o_ref, px, base):
    e = e_ref[base : base + 128].astype(F32)
    o = o_ref[base : base + 128].astype(F32)
    before, after = before_after(px, e, o)
    return jnp.concatenate(
        [planes(before, 8), planes(own.astype(F32), ROWS), planes(after, 8)], axis=1
    )


def edge_y_kernel(s_ref, m_ref, f_ref, xe_ref, xo_ref, ve_ref, vo_ref, e_ref, o_ref):
    px = s_ref[PX]
    py = s_ref[PY]
    row = 0
    for n, (ref, groups) in enumerate(((m_ref, 4), (f_ref, 8))):
        ext = extended(ref[...], xe_ref, xo_ref, px, 128 * n).reshape(DEPTH * EXT, 2 * LANES)
        first = pack_edge(ext[:, :LANES], groups, False)
        last = pack_edge(ext[:, LANES:], groups, True)
        size = first.shape[0]
        e_ref[row : row + size] = pick(py, last, first).astype(BF16)
        o_ref[row : row + size] = pick(py, first, last).astype(BF16)
        row += size
    e_ref[row : row + 384] = ve_ref[...]
    o_ref[row : row + 384] = vo_ref[...]
    row += 384
    before, after = before_after(px, xe_ref[256:272].astype(F32), xo_ref[256:272].astype(F32))
    lane = lane_iota((16, LANES))
    sides = []
    for j in range(2):
        acc = jnp.zeros((16, LANES), F32)
        for c in range(3):
            for i in range(2):
                acc = jnp.where(lane == 2 * c + i, s_ref[OFF + 4 * c + 2 * i + j].astype(F32), acc)
        tissue = (
            before[:, LANES * j : LANES * j + LANES],
            s_ref[TIS + j].astype(F32),
            s_ref[TIS + 2 + j].astype(F32),
            after[:, LANES * j : LANES * j + LANES],
        )
        for i, t in enumerate(tissue):
            acc = jnp.where(lane == 8 + i, t, acc)
        sides.append(acc)
    e_ref[row : row + 16] = pick(py, sides[1], sides[0]).astype(BF16)
    o_ref[row : row + 16] = pick(py, sides[0], sides[1]).astype(BF16)


Y_FIXED, Y_VEL, Y_META, Y_ROWS = 192, 288, 672, 688


def sides_of(py, e_ref, o_ref, start, size):
    e = e_ref[start : start + size].astype(F32)
    o = o_ref[start : start + size].astype(F32)
    left, right = before_after(py, e, o)
    return right, left


def warp_kernel(
    s_ref, m_ref, xe_ref, xo_ref, ye_ref, yo_ref, v_hbm,
    w_ref, slope_ref, e_ref, o_ref,
    m_scr, v_scr, r_scr, sem,
):
    px = s_ref[PX]
    py = s_ref[PY]
    copies = []
    for c in range(3):
        for j in range(2):
            copies.append(
                pltpu.make_async_copy(
                    v_hbm.at[c, :, pl.ds(LANES * j, LANES)], v_scr.at[c, j], sem.at[2 * c + j]
                )
            )
    for copy in copies:
        copy.start()

    zero = jnp.zeros((3 * EXT, LANES), F32)
    for j in range(3):
        m_scr[j, 0 : 3 * EXT] = zero
        m_scr[j, 19 * EXT : 22 * EXT] = zero
    ext = extended(m_ref[...], xe_ref, xo_ref, px, 0).reshape(DEPTH * EXT, 2 * LANES)
    m_scr[0, 3 * EXT : 19 * EXT] = ext[:, :LANES]
    m_scr[1, 3 * EXT : 19 * EXT] = ext[:, LANES:]
    right, left = sides_of(py, ye_ref, yo_ref, 0, 192)
    for k in range(4):
        m_scr[2, 3 * EXT + 192 * k : 3 * EXT + 192 * k + 192] = unpack_group(right, left, k, 4)
    for c in range(3):
        right, left = sides_of(py, ye_ref, yo_ref, Y_VEL + 128 * c, 128)
        right = right[:64] + right[64:]
        left = left[:64] + left[64:]
        for k in range(8):
            v_scr[c, 2, 64 * k : 64 * k + 64] = unpack_group(right, left, k, 8)
    m_right, m_left = sides_of(py, ye_ref, yo_ref, Y_META, 16)
    lane8 = lane_iota((16, LANES))
    first_row = lax.broadcasted_iota(jnp.int32, (16, LANES), 0) == 0

    def scalar(meta, k):
        return jnp.sum(jnp.where(first_row & (lane8 == k), meta, 0.0)).astype(jnp.int32)

    lane = lane_iota((DEPTH, LANES))

    def gather(j, xb, oz, ox, oy, merge):
        shifts = []
        for b in range(2):
            s = oy + b
            nbr = jnp.where(s >= 0, (j + 1) % 3, (j + 2) % 3)
            lo = jnp.where(s >= 0, 0, LANES + s)
            hi = jnp.where(s >= 0, s, LANES)
            mask = (lane >= lo) & (lane < hi)
            shifts.append((nbr, mask, (LANES - s) & (LANES - 1)))
        base = (3 + oz) * EXT + xb * BX + 8 + ox

        @pl.loop(0, BX + 1)
        def _(x):
            for c in range(2):
                start = base + c * EXT + x
                own = m_scr[j, pl.ds(start, DEPTH, stride=EXT), :]
                for b in range(2):
                    nbr, mask, amount = shifts[b]
                    other = m_scr[nbr, pl.ds(start, DEPTH, stride=EXT), :]
                    val = pltpu.roll(jnp.where(mask, other, own), amount, 1)
                    if merge:
                        val = jnp.where(lane < LANES // 2, r_scr[b, c, x], val)
                    r_scr[b, c, x] = val

    def blend(j, xb):
        @pl.loop(0, BX)
        def _(x):
            row = xb * BX + x
            f0, f1, f2 = (v_scr[c, j, pl.ds(row, DEPTH, stride=ROWS), :] for c in range(3))
            mid, dx, dy = [], [], []
            for c in range(2):
                low, dif = [], []
                for a in range(2):
                    s0 = r_scr[0, c, x + a]
                    d = r_scr[1, c, x + a] - s0
                    dif.append(d)
                    low.append(s0 + f2 * d)
                step = low[1] - low[0]
                dx.append(step)
                mid.append(low[0] + f1 * step)
                dy.append(dif[0] + f1 * (dif[1] - dif[0]))
            dz = mid[1] - mid[0]
            lanes = slice(LANES * j, LANES * j + LANES)
            w_ref[row, :, lanes] = (mid[0] + f0 * dz).astype(BF16)
            slope_ref[0, row, :, lanes] = dz
            slope_ref[1, row, :, lanes] = dx[0] + f0 * (dx[1] - dx[0])
            slope_ref[2, row, :, lanes] = dy[0] + f0 * (dy[1] - dy[0])

    for xb in range(2):
        gather(2, xb, *(scalar(m_right, 2 * c + xb) for c in range(3)), False)
        gather(2, xb, *(scalar(m_left, 2 * c + xb) for c in range(3)), True)
        blend(2, xb)
    for copy in copies:
        copy.wait()
    for j in range(2):
        for xb in range(2):
            gather(j, xb, *(s_ref[OFF + 4 * c + 2 * xb + j] for c in range(3)), False)
            blend(j, xb)
    e_ref[...] = w_ref[pl.ds(jnp.where(px == 0, ROWS - 8, 0), 8)]
    o_ref[...] = w_ref[pl.ds(jnp.where(px == 0, 0, ROWS - 8), 8)]


def box_x(load, store, count):
    v, three = {}, {}
    for x in range(count + 8):
        v[x] = load(x)
        if x >= 2:
            three[x - 2] = v[x - 2] + v[x - 1] + v[x]
        if x >= 8:
            store(x - 8, three[x - 8] + three[x - 5] + three[x - 2])


def add_all(terms):
    terms = [t for t in terms if t is not None]
    if not terms:
        return None
    total = terms[0]
    for t in terms[1:]:
        total = total + t
    return total


def box_z(v):
    three = {z: add_all([v[i] for i in (z - 1, z, z + 1) if 0 <= i < DEPTH]) for z in range(-3, 19)}
    return [add_all([three[z - 3], three[z], three[z + 3]]) for z in range(DEPTH)]


def shift_y(v, s):
    lane = lane_iota(v[0].shape)
    if s > 0:
        return [roll(jnp.where(lane < s, v[(j + 1) % 3], v[j]), -s) for j in range(3)]
    return [roll(jnp.where(lane >= LANES + s, v[(j + 2) % 3], v[j]), -s) for j in range(3)]


def box_y(v):
    for s in (1, 3):
        a, b = shift_y(v, s), shift_y(v, -s)
        v = [x + y + z for x, y, z in zip(a, v, b)]
    return v


def fixed_kernel(
    s_ref, f_ref, xe_ref, xo_ref, ye_ref, yo_ref,
    fx_ref, sum_ref, mask_ref,
    f_scr, z_scr, b_scr,
):
    px = s_ref[PX]
    py = s_ref[PY]
    ext = extended(f_ref[...], xe_ref, xo_ref, px, 128).reshape(DEPTH * EXT, 2 * LANES)
    f_scr[0] = ext[:, :LANES]
    f_scr[1] = ext[:, LANES:]
    right, left = sides_of(py, ye_ref, yo_ref, Y_FIXED, 96)
    for k in range(8):
        f_scr[2, 96 * k : 96 * k + 96] = unpack_group(right, left, k, 8)

    before, after = before_after(px, xe_ref[256:264].astype(F32), xo_ref[256:264].astype(F32))
    m_right, m_left = sides_of(py, ye_ref, yo_ref, Y_META, 8)
    row = lax.broadcasted_iota(jnp.int32, (OUT, LANES), 0)
    lane = lane_iota((8, LANES))

    def column(meta, k):
        picked = jnp.sum(jnp.where(lane == 8 + k, meta, 0.0), axis=1, keepdims=True)[:1]
        return jnp.broadcast_to(picked, (1, LANES))

    for j in range(3):
        if j < 2:
            lanes = slice(LANES * j, LANES * j + LANES)
            t = [
                before[:1, lanes],
                jnp.full((1, LANES), s_ref[TIS + j].astype(F32)),
                jnp.full((1, LANES), s_ref[TIS + 2 + j].astype(F32)),
                after[:1, lanes],
            ]
        else:
            half = lane_iota((1, LANES)) < LANES // 2
            t = [jnp.where(half, column(m_right, k), column(m_left, k)) for k in range(4)]
        mask_ref[j] = jnp.where(row < 4, t[0], jnp.where(row < 20, t[1], jnp.where(row < 36, t[2], t[3])))

    @pl.loop(0, 3)
    def _(j):
        def load(x):
            return f_scr[j, pl.ds(x, DEPTH, stride=EXT), :]

        for q in range(2):
            def value(x):
                v = load(x)
                if q == 0:
                    fx_ref[x, j] = v.astype(BF16)
                return v if q == 0 else v * v

            def store(x, v):
                z_scr[q, j, pl.ds(x, DEPTH, stride=OUT), :] = v

            box_x(value, store, OUT)

    sum_zy(z_scr, b_scr, 2, lambda z, at, sums: put_sums(sum_ref, at, sums))


def put_sums(ref, at, sums):
    for q, v in enumerate(sums):
        for j in range(3):
            ref[q, j, pl.ds(at, 8), :] = v[j]


def sum_zy(z_scr, b_scr, count, use):
    @pl.loop(0, OUT // 8)
    def _(t):
        def at(z):
            return pl.multiple_of(z * OUT + t * 8, 8)

        for q in range(count):
            for j in range(3):
                v = box_z([z_scr[q, j, pl.ds(at(z), 8), :] for z in range(DEPTH)])
                for z in range(DEPTH):
                    b_scr[q, j, z] = v[z]

        @pl.loop(0, DEPTH)
        def _(z):
            use(t, at(z), [box_y([b_scr[q, j, z] for j in range(3)]) for q in range(count)])


def gradient_kernel(
    s_ref, w_ref, we_ref, wo_ref, fx_ref, sum_ref, mask_ref, slope_ref, gh_ref, gl_ref,
    ys_ref, e_ref, o_ref, loss_ref,
    i_scr, z_scr, b_scr, a_scr, g_scr,
):
    px = s_ref[PX]
    before, after = before_after(px, we_ref[...].astype(F32), wo_ref[...].astype(F32))
    for j in range(3):
        lanes = slice(LANES * j, LANES * j + LANES)
        i_scr[0:8, j] = before[:, :, lanes]
        i_scr[8:40, j] = w_ref[:, :, lanes].astype(F32)
        i_scr[40:48, j] = after[:, :, lanes]

    @pl.loop(0, 3)
    def _(j):
        for q in range(3):
            def value(x):
                v = i_scr[x, j]
                if q == 0:
                    return v
                return v * (v if q == 1 else fx_ref[x, j].astype(F32))

            def store(x, v):
                z_scr[q, j, pl.ds(x, DEPTH, stride=OUT), :] = v

            box_x(value, store, OUT)

    loss_ref[...] = jnp.zeros((8, LANES), F32)
    rows8 = lax.broadcasted_iota(jnp.int32, (8, LANES), 0)

    def stats(t, at, sums):
        inner = (rows8 + t * 8 >= 4) & (rows8 + t * 8 < 4 + ROWS)
        total = None
        for j in range(3):
            si, sii, sij = (sums[q][j] for q in range(3))
            sj = sum_ref[0, j, pl.ds(at, 8), :]
            sjj = sum_ref[1, j, pl.ds(at, 8), :]
            m = mask_ref[j, pl.ds(pl.multiple_of(t * 8, 8), 8), :]
            cross = sij - si * sj * (1.0 / WINDOW_COUNT)
            var_i = sii - si * si * (1.0 / WINDOW_COUNT)
            var_j = sjj - sj * sj * (1.0 / WINDOW_COUNT)
            quotient = cross / (var_i * var_j + VAR_EPSILON)
            second = quotient * quotient * var_j
            a_scr[0, j, pl.ds(at, 8), :] = (2.0 / WINDOW_COUNT) * m * (quotient * sj - second * si)
            a_scr[1, j, pl.ds(at, 8), :] = m * second
            a_scr[2, j, pl.ds(at, 8), :] = -2.0 * m * quotient
            if j < 2:
                ncc = jnp.where(inner, m * (cross * quotient), 0.0)
                total = ncc if total is None else total + ncc
        loss_ref[...] += total

    sum_zy(z_scr, b_scr, 3, stats)
    sum_zy(a_scr, b_scr, 3, lambda t, at, sums: put_sums(z_scr, at, sums))

    lane = lane_iota((DEPTH, LANES))
    has_r = s_ref[HAS_R]
    has_l = s_ref[HAS_L]
    r_lim = jnp.where(has_r == 1, GAUSS_RADIUS, 0)
    l_lim = jnp.where(has_l == 1, LANES - GAUSS_RADIUS, LANES)
    valid = (lane < r_lim) | (lane >= l_lim)

    for j in range(3):
        lanes = slice(LANES * j, LANES * j + LANES)
        for q in range(3):
            def load(x):
                return z_scr[q, j, pl.ds(x, DEPTH, stride=OUT), :]

            def store(x, v):
                if q == 0:
                    g_scr[0, x, :, lanes] = v
                elif q == 1:
                    g_scr[0, x, :, lanes] += 2.0 * i_scr[x + 8, j] * v
                else:
                    grad = g_scr[0, x, :, lanes] + fx_ref[x + 8, j].astype(F32) * v
                    for c in (2, 1, 0):
                        val = grad * slope_ref[c, x, :, lanes]
                        if j == 2:
                            val = jnp.where(valid, val, 0.0)
                        g_scr[c, x, :, lanes] = val

            box_x(load, store, ROWS)

    gh = gh_ref[...]
    gl = gl_ref[...]
    for c in range(3):
        g = g_scr[c].reshape(ROWS * DEPTH, 3 * LANES)
        hi = g.astype(BF16)
        lo = (g - hi.astype(F32)).astype(BF16)
        ys = jnp.dot(hi, gh, preferred_element_type=F32)
        ys = ys + jnp.dot(lo, gh, preferred_element_type=F32)
        ys = ys + jnp.dot(hi, gl, preferred_element_type=F32)
        ys = ys.reshape(ROWS, DEPTH, 2 * LANES)
        ys_ref[c] = ys
        first = ys[:GAUSS_RADIUS]
        last = ys[ROWS - GAUSS_RADIUS :]
        e_ref[c] = pick(px, last, first).astype(BF16)
        o_ref[c] = pick(px, first, last).astype(BF16)


def smooth_kernel(s_ref, ys_ref, ge_ref, go_ref, out_hbm, h_scr, z_scr, o_scr, sem):
    weights = gauss_weights()
    px = s_ref[PX]
    r = GAUSS_RADIUS
    for c in range(3):
        before, after = before_after(px, ge_ref[c].astype(F32), go_ref[c].astype(F32))
        h_scr[0, c] = before
        h_scr[1, c] = after
    copies = []
    for c in range(3):
        for j in range(2):
            lanes = slice(LANES * j, LANES * j + LANES)

            def load(x):
                if x < r:
                    return h_scr[0, c, x, :, lanes]
                if x < r + ROWS:
                    return ys_ref[c, x - r, :, lanes]
                return h_scr[1, c, x - r - ROWS, :, lanes]

            for x in range(ROWS):
                total = (-STEP_RATE * weights[r]) * load(x + r)
                for k in range(1, r + 1):
                    total = total + (-STEP_RATE * weights[r + k]) * (load(x + r - k) + load(x + r + k))
                z_scr[pl.ds(x, DEPTH, stride=ROWS), :] = total

            @pl.loop(0, ROWS // 8)
            def _(t):
                def at(z):
                    return pl.multiple_of(z * ROWS + t * 8, 8)

                v = [z_scr[pl.ds(at(z), 8), :] for z in range(DEPTH)]
                for z in range(DEPTH):
                    total = weights[r] * v[z]
                    for k in range(1, r + 1):
                        pair = add_all([v[i] for i in (z - k, z + k) if 0 <= i < DEPTH])
                        if pair is not None:
                            total = total + weights[r + k] * pair
                    o_scr[c, j, pl.ds(at(z), 8), :] = total

            copy = pltpu.make_async_copy(
                o_scr.at[c, j], out_hbm.at[c, :, pl.ds(LANES * j, LANES)], sem.at[2 * c + j]
            )
            copy.start()
            copies.append(copy)
    for copy in copies:
        copy.wait()


def call(kernel, outs, in_specs, out_specs, scratch=()):
    return pl.pallas_call(
        kernel,
        out_shape=tuple(jax.ShapeDtypeStruct(s, d) for s, d in outs),
        in_specs=list(in_specs),
        out_specs=tuple(out_specs),
        scratch_shapes=list(scratch),
        name=kernel.__name__,
    )


def swap(axis, even, odd):
    count = lax.axis_size(axis)
    first = [(i, i ^ 1) for i in range(count) if i ^ 1 < count]
    second = []
    for i in range(1, count - 1, 2):
        second += [(i, i + 1), (i + 1, i)]
    return lax.ppermute(even, axis, first), lax.ppermute(odd, axis, second)


def gauss_matrices():
    weights = gauss_weights()
    g = np.zeros((3 * LANES, 2 * LANES), np.float32)
    for col in range(2 * LANES):
        for tap in range(-GAUSS_RADIUS, GAUSS_RADIUS + 1):
            g[(col + tap) % (3 * LANES), col] = weights[tap + GAUSS_RADIUS]
    hi = jnp.asarray(g).astype(BF16)
    lo = (jnp.asarray(g) - hi.astype(F32)).astype(BF16)
    return hi, lo


def on_device(moving_image, fixed_image, velocity, offsets, tissue):
    ix, iy = lax.axis_index("gx"), lax.axis_index("gy")
    ny = lax.axis_size("gy")
    table = jnp.concatenate(
        [
            jnp.stack([ix & 1, iy & 1, (iy > 0).astype(jnp.int32), (iy < ny - 1).astype(jnp.int32)]),
            offsets.reshape(12),
            tissue.reshape(4),
        ]
    ).astype(jnp.int32)
    rows = DEPTH * ROWS
    m = moving_image.reshape(rows, 2 * LANES)
    f = fixed_image.reshape(rows, 2 * LANES)
    v = velocity.reshape(3, rows, 2 * LANES)

    V, S, A = VMEM_SPEC, SMEM_SPEC, ANY_SPEC
    edge = ((272, 2 * LANES), BF16)
    xe, xo = call(edge_x_kernel, [edge, edge], [S, V, V], [V, V])(table, m, f)
    rxe, rxo = swap("gx", xe, xo)
    edge = ((384, LANES), BF16)
    ve, vo = call(edge_v_kernel, [edge, edge], [S, V], [V, V])(table, v)
    edge = ((Y_ROWS, LANES), BF16)
    ye, yo = call(edge_y_kernel, [edge, edge], [S] + [V] * 6, [V, V])(table, m, f, rxe, rxo, ve, vo)
    rye, ryo = swap("gy", ye, yo)

    edge = ((8, DEPTH, 3 * LANES), BF16)
    w, slope, we, wo = call(
        warp_kernel,
        [((ROWS, DEPTH, 3 * LANES), BF16), ((3, ROWS, DEPTH, 3 * LANES), F32), edge, edge],
        [S] + [V] * 5 + [A],
        [V] * 4,
        [
            pltpu.VMEM((3, 22 * EXT, LANES), F32),
            pltpu.VMEM((3, 3, rows, LANES), F32),
            pltpu.VMEM((2, 2, BX + 1, DEPTH, LANES), F32),
            pltpu.SemaphoreType.DMA((6,)),
        ],
    )(table, m, rxe, rxo, rye, ryo, v)
    rwe, rwo = swap("gx", we, wo)

    fx, sums, mask = call(
        fixed_kernel,
        [((EXT, 3, DEPTH, LANES), BF16), ((2, 3, DEPTH * OUT, LANES), F32), ((3, OUT, LANES), F32)],
        [S] + [V] * 5,
        [V] * 3,
        [
            pltpu.VMEM((3, DEPTH * EXT, LANES), F32),
            pltpu.VMEM((2, 3, DEPTH * OUT, LANES), F32),
            pltpu.VMEM((2, 3, DEPTH, 8, LANES), F32),
        ],
    )(table, f, rxe, rxo, rye, ryo)

    gh, gl = gauss_matrices()
    edge = ((3, GAUSS_RADIUS, DEPTH, 2 * LANES), BF16)
    ys, ge, go, loss = call(
        gradient_kernel,
        [((3, ROWS, DEPTH, 2 * LANES), F32), edge, edge, ((8, LANES), F32)],
        [S] + [V] * 9,
        [V] * 4,
        [
            pltpu.VMEM((EXT, 3, DEPTH, LANES), F32),
            pltpu.VMEM((3, 3, DEPTH * OUT, LANES), F32),
            pltpu.VMEM((3, 3, DEPTH, 8, LANES), F32),
            pltpu.VMEM((3, 3, DEPTH * OUT, LANES), F32),
            pltpu.VMEM((3, ROWS, DEPTH, 3 * LANES), F32),
        ],
    )(table, w, rwe, rwo, fx, sums, mask, slope, gh, gl)
    rge, rgo = swap("gx", ge, go)

    devices = lax.axis_size("gx") * ny
    local = jnp.stack([jnp.sum(loss), jnp.sum(tissue).astype(F32)])
    line = jnp.pad(local, (0, LANES - 2)).reshape(1, 1, LANES)
    everyone = lax.all_to_all(jnp.broadcast_to(line, (devices, 1, LANES)), ("gx", "gy"), 0, 0)
    totals = jnp.sum(everyone, axis=(0, 1))
    similarity_loss = -totals[0] / (totals[1] * float(BX * BY * DEPTH))

    (update,) = call(
        smooth_kernel,
        [((3, rows, 2 * LANES), F32)],
        [S] + [V] * 3,
        [A],
        [
            pltpu.VMEM((2, 3, GAUSS_RADIUS, DEPTH, 2 * LANES), F32),
            pltpu.VMEM((rows, LANES), F32),
            pltpu.VMEM((3, 2, rows, LANES), F32),
            pltpu.SemaphoreType.DMA((6,)),
        ],
    )(table, ys, rge, rgo)
    return update.reshape(velocity.shape), similarity_loss


def solution(mesh):
    in_specs = (
        P(None, "gx", "gy"),
        P(None, "gx", "gy"),
        P(None, None, "gx", "gy"),
        P(None, "gx", "gy"),
        P("gx", "gy"),
    )
    out_specs = (P(None, None, "gx", "gy"), P())
    return jax.shard_map(
        on_device, mesh=mesh, in_specs=in_specs, out_specs=out_specs, check_vma=False
    )
```

```python
import functools
import math

import jax
import jax.numpy as jnp
import numpy as np
from jax import lax
from jax.experimental import pallas as pl
from jax.experimental.pallas import tpu as pltpu
from jax.sharding import PartitionSpec as P

DEPTH = 16
BX = 16
BY = 128
ROWS = 32
EXT = 48
OUT = 40
LANES = 128
GAUSS_RADIUS = 7
BOX_RADIUS = 4
GAUSS_SIGMA = 3.0
WINDOW_COUNT = 729.0
VAR_EPSILON = 1e-05
STEP_RATE = 16.0
F32 = jnp.float32
BF16 = jnp.bfloat16

VMEM_SPEC = pl.BlockSpec(memory_space=pltpu.VMEM)
SMEM_SPEC = pl.BlockSpec(memory_space=pltpu.SMEM)
ANY_SPEC = pl.BlockSpec(memory_space=pl.ANY)

PX, PY, HAS_L, HAS_R, OFF, TIS = 0, 1, 2, 3, 4, 16


def gauss_weights():
    raw = [
        math.exp(-float(tap * tap) / (2.0 * GAUSS_SIGMA * GAUSS_SIGMA))
        for tap in range(-GAUSS_RADIUS, GAUSS_RADIUS + 1)
    ]
    total = sum(raw)
    return [w / total for w in raw]


def unrolled(count):
    def run(body):
        for i in range(count):
            body(i)

    return run


def lane_iota(shape):
    return lax.broadcasted_iota(jnp.int32, shape, len(shape) - 1)


def roll(x, shift):
    shift = shift % LANES
    return x if shift == 0 else pltpu.roll(x, shift, len(x.shape) - 1)


def pack_edge(tile, groups, last):
    rows = tile.shape[0] // groups
    width = LANES // groups
    lane = lane_iota((rows, LANES))
    acc = None
    for k in range(groups):
        piece = roll(tile[k * rows : (k + 1) * rows], width * (k + 1) if last else width * k)
        acc = piece if acc is None else jnp.where(lane // width == k, piece, acc)
    return acc


def unpack_group(right, left, k, groups):
    width = LANES // groups
    r = roll(right, -width * k)
    l = roll(left, -width * (k + 1))
    return jnp.where(lane_iota(r.shape) < LANES // 2, r, l)


def pick(flag, a, b):
    return jnp.where(flag == 0, a, b)


def planes(x, rows):
    return x.reshape(DEPTH, rows, x.shape[-1])


def edge_x_kernel(s_ref, m_ref, f_ref, e_ref, o_ref):
    px = s_ref[PX]
    lane = lane_iota((16, 2 * LANES))
    for n, ref in enumerate((m_ref, f_ref)):
        v = planes(ref[...].astype(F32), ROWS)
        first = v[:, :8].reshape(128, 2 * LANES)
        last = v[:, 24:].reshape(128, 2 * LANES)
        e_ref[128 * n : 128 * n + 128] = pick(px, last, first).astype(BF16)
        o_ref[128 * n : 128 * n + 128] = pick(px, first, last).astype(BF16)
    t = [[s_ref[TIS + 2 * i + j].astype(F32) for j in range(2)] for i in range(2)]
    first = jnp.where(lane < LANES, t[0][0], t[0][1])
    last = jnp.where(lane < LANES, t[1][0], t[1][1])
    e_ref[256:272] = pick(px, last, first).astype(BF16)
    o_ref[256:272] = pick(px, first, last).astype(BF16)


def edge_v_kernel(s_ref, v_ref, e_ref, o_ref):
    py = s_ref[PY]
    for c in range(3):
        first = pack_edge(v_ref[c, :, :LANES], 8, False)
        last = pack_edge(v_ref[c, :, LANES:], 8, True)
        for ref, val in ((e_ref, pick(py, last, first)), (o_ref, pick(py, first, last))):
            hi = val.astype(BF16)
            ref[128 * c : 128 * c + 64] = hi
            ref[128 * c + 64 : 128 * c + 128] = (val - hi.astype(F32)).astype(BF16)


def before_after(px, e, o):
    return pick(px, o, e), pick(px, e, o)


def extended(own, e_ref, o_ref, px, base):
    e = e_ref[base : base + 128].astype(F32)
    o = o_ref[base : base + 128].astype(F32)
    before, after = before_after(px, e, o)
    return jnp.concatenate(
        [planes(before, 8), planes(own.astype(F32), ROWS), planes(after, 8)], axis=1
    )


def edge_y_kernel(s_ref, m_ref, f_ref, xe_ref, xo_ref, ve_ref, vo_ref, e_ref, o_ref):
    px = s_ref[PX]
    py = s_ref[PY]
    row = 0
    for n, (ref, groups) in enumerate(((m_ref, 4), (f_ref, 8))):
        ext = extended(ref[...], xe_ref, xo_ref, px, 128 * n).reshape(DEPTH * EXT, 2 * LANES)
        first = pack_edge(ext[:, :LANES], groups, False)
        last = pack_edge(ext[:, LANES:], groups, True)
        size = first.shape[0]
        e_ref[row : row + size] = pick(py, last, first).astype(BF16)
        o_ref[row : row + size] = pick(py, first, last).astype(BF16)
        row += size
    e_ref[row : row + 384] = ve_ref[...]
    o_ref[row : row + 384] = vo_ref[...]
    row += 384
    before, after = before_after(px, xe_ref[256:272].astype(F32), xo_ref[256:272].astype(F32))
    lane = lane_iota((16, LANES))
    sides = []
    for j in range(2):
        acc = jnp.zeros((16, LANES), F32)
        for c in range(3):
            for i in range(2):
                acc = jnp.where(lane == 2 * c + i, s_ref[OFF + 4 * c + 2 * i + j].astype(F32), acc)
        tissue = (
            before[:, LANES * j : LANES * j + LANES],
            s_ref[TIS + j].astype(F32),
            s_ref[TIS + 2 + j].astype(F32),
            after[:, LANES * j : LANES * j + LANES],
        )
        for i, t in enumerate(tissue):
            acc = jnp.where(lane == 8 + i, t, acc)
        sides.append(acc)
    e_ref[row : row + 16] = pick(py, sides[1], sides[0]).astype(BF16)
    o_ref[row : row + 16] = pick(py, sides[0], sides[1]).astype(BF16)


Y_FIXED, Y_VEL, Y_META, Y_ROWS = 192, 288, 672, 688


def sides_of(py, e_ref, o_ref, start, size):
    e = e_ref[start : start + size].astype(F32)
    o = o_ref[start : start + size].astype(F32)
    left, right = before_after(py, e, o)
    return right, left


def warp_kernel(
    s_ref, m_ref, xe_ref, xo_ref, ye_ref, yo_ref, v_hbm,
    w_ref, slope_ref, e_ref, o_ref,
    m_scr, v_scr, r_scr, sem,
):
    px = s_ref[PX]
    py = s_ref[PY]
    copies = []
    for c in range(3):
        for j in range(2):
            copies.append(
                pltpu.make_async_copy(
                    v_hbm.at[c, :, pl.ds(LANES * j, LANES)], v_scr.at[c, j], sem.at[2 * c + j]
                )
            )
    for copy in copies:
        copy.start()

    zero = jnp.zeros((3 * EXT, LANES), F32)
    for j in range(3):
        m_scr[j, 0 : 3 * EXT] = zero
        m_scr[j, 19 * EXT : 22 * EXT] = zero
    ext = extended(m_ref[...], xe_ref, xo_ref, px, 0).reshape(DEPTH * EXT, 2 * LANES)
    m_scr[0, 3 * EXT : 19 * EXT] = ext[:, :LANES]
    m_scr[1, 3 * EXT : 19 * EXT] = ext[:, LANES:]
    right, left = sides_of(py, ye_ref, yo_ref, 0, 192)
    for k in range(4):
        m_scr[2, 3 * EXT + 192 * k : 3 * EXT + 192 * k + 192] = unpack_group(right, left, k, 4)
    for c in range(3):
        right, left = sides_of(py, ye_ref, yo_ref, Y_VEL + 128 * c, 128)
        right = right[:64] + right[64:]
        left = left[:64] + left[64:]
        for k in range(8):
            v_scr[c, 2, 64 * k : 64 * k + 64] = unpack_group(right, left, k, 8)
    digit = lax.broadcasted_iota(jnp.int32, (16, LANES), 1)
    power = (1 << (4 * jnp.minimum(digit, 5))).astype(F32)
    use = (lax.broadcasted_iota(jnp.int32, (16, LANES), 0) == 0) & (digit < 6)

    def offsets_of(meta):
        code = jnp.sum(jnp.where(use, (meta + 8.0) * power, 0.0)).astype(jnp.int32)
        return [((code >> (4 * k)) & 15) - 8 for k in range(6)]

    m_right, m_left = (offsets_of(x) for x in sides_of(py, ye_ref, yo_ref, Y_META, 16))
    lane = lane_iota((DEPTH, LANES))

    def gather(j, xb, oz, ox, oy, merge):
        shifts = []
        for b in range(2):
            s = oy + b
            nbr = jnp.where(s >= 0, (j + 1) % 3, (j + 2) % 3)
            lo = jnp.where(s >= 0, 0, LANES + s)
            hi = jnp.where(s >= 0, s, LANES)
            mask = (lane >= lo) & (lane < hi)
            shifts.append((nbr, mask, (LANES - s) & (LANES - 1)))
        base = (3 + oz) * EXT + xb * BX + 8 + ox

        @unrolled(BX + 1)
        def _(x):
            for c in range(2):
                start = base + c * EXT + x
                own = m_scr[j, pl.ds(start, DEPTH, stride=EXT), :]
                for b in range(2):
                    nbr, mask, amount = shifts[b]
                    other = m_scr[nbr, pl.ds(start, DEPTH, stride=EXT), :]
                    val = pltpu.roll(jnp.where(mask, other, own), amount, 1)
                    if merge:
                        val = jnp.where(lane < LANES // 2, r_scr[b, c, x], val)
                    r_scr[b, c, x] = val

    def blend(j, xb):
        @pl.loop(0, BX, unroll=4)
        def _(x):
            row = xb * BX + x
            f0, f1, f2 = (v_scr[c, j, pl.ds(row, DEPTH, stride=ROWS), :] for c in range(3))
            mid, dx, dy = [], [], []
            for c in range(2):
                low, dif = [], []
                for a in range(2):
                    s0 = r_scr[0, c, x + a]
                    d = r_scr[1, c, x + a] - s0
                    dif.append(d)
                    low.append(s0 + f2 * d)
                step = low[1] - low[0]
                dx.append(step)
                mid.append(low[0] + f1 * step)
                dy.append(dif[0] + f1 * (dif[1] - dif[0]))
            dz = mid[1] - mid[0]
            lanes = slice(LANES * j, LANES * j + LANES)
            w_ref[row, :, lanes] = (mid[0] + f0 * dz).astype(BF16)
            slope_ref[0, row, :, lanes] = dz
            slope_ref[1, row, :, lanes] = dx[0] + f0 * (dx[1] - dx[0])
            slope_ref[2, row, :, lanes] = dy[0] + f0 * (dy[1] - dy[0])

    for xb in range(2):
        gather(2, xb, *(m_right[2 * c + xb] for c in range(3)), False)
        gather(2, xb, *(m_left[2 * c + xb] for c in range(3)), True)
        blend(2, xb)
    for copy in copies:
        copy.wait()
    for j in range(2):
        for xb in range(2):
            gather(j, xb, *(s_ref[OFF + 4 * c + 2 * xb + j] for c in range(3)), False)
            blend(j, xb)
    e_ref[...] = w_ref[pl.ds(jnp.where(px == 0, ROWS - 8, 0), 8)]
    o_ref[...] = w_ref[pl.ds(jnp.where(px == 0, 0, ROWS - 8), 8)]


def box_x(load, store, count):
    v, three = {}, {}
    for x in range(count + 8):
        v[x] = load(x)
        if x >= 2:
            three[x - 2] = v[x - 2] + v[x - 1] + v[x]
        if x >= 8:
            store(x - 8, three[x - 8] + three[x - 5] + three[x - 2])


def add_all(terms):
    terms = [t for t in terms if t is not None]
    if not terms:
        return None
    total = terms[0]
    for t in terms[1:]:
        total = total + t
    return total


def box_z(v):
    three = {z: add_all([v[i] for i in (z - 1, z, z + 1) if 0 <= i < DEPTH]) for z in range(-3, 19)}
    return [add_all([three[z - 3], three[z], three[z + 3]]) for z in range(DEPTH)]


def split(v):
    hi = v.astype(BF16)
    return hi, (v - hi.astype(F32)).astype(BF16)


def dot(a, b):
    return jnp.dot(a, b, preferred_element_type=F32)


def box_y(parts, band):
    total = None
    for p in parts:
        d = dot(p, band)
        total = d if total is None else total + d
    return total


def put_tiles(ref, q, first, v):
    for j in range(3):
        ref[q, j, pl.ds(first, v.shape[0]), :] = v[:, LANES * j : LANES * j + LANES]


def box_z_in_place(ref, q, count):
    @pl.loop(0, count // 8)
    def _(t):
        for j in range(3):
            rows = [pl.ds(t * 128 + z, 8, stride=DEPTH) for z in range(DEPTH)]
            v = box_z([ref[q, j, r, :] for r in rows])
            for z in range(DEPTH):
                ref[q, j, rows[z], :] = v[z]


def window_kernel(
    s_ref, f_ref, xe_ref, xo_ref, ye_ref, yo_ref, w_ref, band_ref,
    fx_ref, sum_ref, mask_ref, own_ref,
    f_scr, y_scr,
):
    px = s_ref[PX]
    py = s_ref[PY]
    ext = extended(f_ref[...], xe_ref, xo_ref, px, 128).reshape(DEPTH * EXT, 2 * LANES)
    f_scr[0] = ext[:, :LANES]
    f_scr[1] = ext[:, LANES:]
    right, left = sides_of(py, ye_ref, yo_ref, Y_FIXED, 96)
    for k in range(8):
        f_scr[2, 96 * k : 96 * k + 96] = unpack_group(right, left, k, 8)

    before, after = before_after(px, xe_ref[256:264].astype(F32), xo_ref[256:264].astype(F32))
    m_right, m_left = sides_of(py, ye_ref, yo_ref, Y_META, 8)
    row = lax.broadcasted_iota(jnp.int32, (OUT, LANES), 0)
    lane = lane_iota((8, LANES))

    def column(meta, k):
        picked = jnp.sum(jnp.where(lane == 8 + k, meta, 0.0), axis=1, keepdims=True)[:1]
        return jnp.broadcast_to(picked, (1, LANES))

    for j in range(3):
        if j < 2:
            lanes = slice(LANES * j, LANES * j + LANES)
            t = [
                before[:1, lanes],
                jnp.full((1, LANES), s_ref[TIS + j].astype(F32)),
                jnp.full((1, LANES), s_ref[TIS + 2 + j].astype(F32)),
                after[:1, lanes],
            ]
        else:
            half = lane_iota((1, LANES)) < LANES // 2
            t = [jnp.where(half, column(m_right, k), column(m_left, k)) for k in range(4)]
        mask_ref[j] = jnp.where(row < 4, t[0], jnp.where(row < 20, t[1], jnp.where(row < 36, t[2], t[3])))

    for x in range(EXT):
        for j in range(3):
            v = f_scr[j, pl.ds(x, DEPTH, stride=EXT), :]
            fx_ref[x, :, LANES * j : LANES * j + LANES] = v.astype(BF16)

    band = band_ref[...]
    for part in range(3):
        x = 16 * part
        f = fx_ref[x : x + 16].reshape(256, 3 * LANES)
        v = f.astype(F32)
        put_tiles(y_scr, 0, 256 * part, box_y([f], band))
        put_tiles(y_scr, 1, 256 * part, box_y(split(v * v), band))
    for part in range(2):
        x = 16 * part
        w = w_ref[x : x + 16].reshape(256, 3 * LANES)
        f = fx_ref[x + 8 : x + 24].reshape(256, 3 * LANES)
        image_sums(own_ref, 256 * part, w, f, band)
    for q in range(2):
        box_z_in_place(y_scr, q, EXT)
        for j in range(3):
            def load(x):
                return y_scr[q, j, DEPTH * x : DEPTH * x + DEPTH]

            def store(x, v):
                sum_ref[q, j, DEPTH * x : DEPTH * x + DEPTH] = v

            box_x(load, store, OUT)
    for q in range(3):
        box_z_in_place(own_ref, q, ROWS)


def image_sums(ref, first, w, f, band):
    i = w.astype(F32)
    put_tiles(ref, 0, first, box_y([w], band))
    put_tiles(ref, 1, first, box_y(split(i * i), band))
    put_tiles(ref, 2, first, box_y(split(i * f.astype(F32)), band))


def gradient_kernel(
    s_ref, w_ref, we_ref, wo_ref, fx_ref, sum_ref, mask_ref, own_ref, slope_ref,
    band_ref, gh_ref, gl_ref,
    ys_ref, e_ref, o_ref, loss_ref,
    h_scr, s_scr, a_scr, b_scr,
):
    px = s_ref[PX]
    band = band_ref[...]
    before, after = before_after(px, we_ref[...].astype(F32), wo_ref[...].astype(F32))
    w = jnp.concatenate([before, after], axis=0).astype(BF16).reshape(256, 3 * LANES)
    f = jnp.concatenate([fx_ref[0:8], fx_ref[40:48]], axis=0).reshape(256, 3 * LANES)
    image_sums(h_scr, 0, w, f, band)
    for q in range(3):
        box_z_in_place(h_scr, q, 16)

    @pl.loop(0, 3)
    def _(j):
        for q in range(3):
            def load(x):
                if 8 <= x < 40:
                    return own_ref[q, j, DEPTH * (x - 8) : DEPTH * (x - 7)]
                x = x if x < 8 else x - 32
                return h_scr[q, j, DEPTH * x : DEPTH * x + DEPTH]

            def store(x, v):
                s_scr[q, j, DEPTH * x : DEPTH * x + DEPTH] = v

            box_x(load, store, OUT)

    lane = lane_iota((DEPTH, LANES))
    near = (lane < 11) | (lane >= LANES - 11)

    def stats(x, inner):
        total = None
        first = x * DEPTH
        rows = pl.ds(pl.multiple_of(first, DEPTH) if inner else first, DEPTH)
        for j in range(3):
            si, sii, sij = (s_scr[q, j, rows, :] for q in range(3))
            sj = sum_ref[0, j, rows, :]
            sjj = sum_ref[1, j, rows, :]
            m = jnp.broadcast_to(mask_ref[j, pl.ds(x, 1), :], (DEPTH, LANES))
            cross = sij - si * sj * (1.0 / WINDOW_COUNT)
            var_i = sii - si * si * (1.0 / WINDOW_COUNT)
            var_j = sjj - sj * sj * (1.0 / WINDOW_COUNT)
            quotient = cross / (var_i * var_j + VAR_EPSILON)
            second = quotient * quotient * var_j
            adjoint = (
                (2.0 / WINDOW_COUNT) * m * (quotient * sj - second * si),
                m * second,
                -2.0 * m * quotient,
            )
            for k in range(3):
                a_scr[k, j, rows, :] = adjoint[k] if j < 2 else jnp.where(near, adjoint[k], 0.0)
            if inner and j < 2:
                ncc = m * (cross * quotient)
                total = ncc if total is None else total + ncc
        if inner:
            loss_ref[...] += total

    loss_ref[...] = jnp.zeros((DEPTH, LANES), F32)

    @pl.loop(0, ROWS, unroll=2)
    def _(x):
        stats(x + 4, True)

    for x in (0, 1, 2, 3, 36, 37, 38, 39):
        stats(x, False)

    for k in range(3):
        box_z_in_place(a_scr, k, OUT)

    for j in range(3):
        lanes = slice(LANES * j, LANES * j + LANES)
        for k in range(3):
            def load(x):
                return a_scr[k, j, DEPTH * x : DEPTH * x + DEPTH]

            def store(x, v):
                hi, lo = split(v)
                b_scr[k, 0, x, :, lanes] = hi
                b_scr[k, 1, x, :, lanes] = lo

            box_x(load, store, ROWS)

    column = lane_iota((1, 3 * LANES))
    r_lim = jnp.where(s_ref[HAS_R] == 1, 2 * LANES + GAUSS_RADIUS, 2 * LANES)
    l_lim = jnp.where(s_ref[HAS_L] == 1, 3 * LANES - GAUSS_RADIUS, 3 * LANES)
    valid = (column < r_lim) | (column >= l_lim)
    gh = gh_ref[...]
    gl = gl_ref[...]
    for part in range(2):
        x = 16 * part

        def flat(v):
            return v.reshape(256, 3 * LANES)

        spread = [
            box_y([flat(b_scr[k, i, x : x + 16]) for i in range(2)], band) for k in range(3)
        ]
        i = flat(w_ref[x : x + 16]).astype(F32)
        t = flat(fx_ref[x + 8 : x + 24]).astype(F32)
        grad = spread[0] + 2.0 * i * spread[1] + t * spread[2]
        for c in range(3):
            g = jnp.where(valid, grad * flat(slope_ref[c, x : x + 16]), 0.0)
            hi, lo = split(g)
            ys = dot(hi, gh) + dot(lo, gh) + dot(hi, gl)
            ys_ref[c, x : x + 16] = ys.reshape(16, DEPTH, 2 * LANES)
    for c in range(3):
        first = ys_ref[c, :GAUSS_RADIUS]
        last = ys_ref[c, ROWS - GAUSS_RADIUS :]
        e_ref[c] = pick(px, last, first).astype(BF16)
        o_ref[c] = pick(px, first, last).astype(BF16)


def smooth_kernel(s_ref, ys_ref, ge_ref, go_ref, out_hbm, h_scr, z_scr, o_scr, sem):
    weights = gauss_weights()
    px = s_ref[PX]
    r = GAUSS_RADIUS
    for c in range(3):
        before, after = before_after(px, ge_ref[c].astype(F32), go_ref[c].astype(F32))
        h_scr[0, c] = before
        h_scr[1, c] = after
    copies = []
    for c in range(3):
        for j in range(2):
            lanes = slice(LANES * j, LANES * j + LANES)

            def load(x):
                if x < r:
                    return h_scr[0, c, x, :, lanes]
                if x < r + ROWS:
                    return ys_ref[c, x - r, :, lanes]
                return h_scr[1, c, x - r - ROWS, :, lanes]

            for x in range(ROWS):
                total = (-STEP_RATE * weights[r]) * load(x + r)
                for k in range(1, r + 1):
                    total = total + (-STEP_RATE * weights[r + k]) * (load(x + r - k) + load(x + r + k))
                z_scr[pl.ds(x, DEPTH, stride=ROWS), :] = total

            @pl.loop(0, ROWS // 8)
            def _(t):
                def at(z):
                    return pl.multiple_of(z * ROWS + t * 8, 8)

                v = [z_scr[pl.ds(at(z), 8), :] for z in range(DEPTH)]
                for z in range(DEPTH):
                    total = weights[r] * v[z]
                    for k in range(1, r + 1):
                        pair = add_all([v[i] for i in (z - k, z + k) if 0 <= i < DEPTH])
                        if pair is not None:
                            total = total + weights[r + k] * pair
                    o_scr[c, j, pl.ds(at(z), 8), :] = total

            copy = pltpu.make_async_copy(
                o_scr.at[c, j], out_hbm.at[c, :, pl.ds(LANES * j, LANES)], sem.at[2 * c + j]
            )
            copy.start()
            copies.append(copy)
    for copy in copies:
        copy.wait()


def call(kernel, outs, in_specs, out_specs, scratch=()):
    return pl.pallas_call(
        kernel,
        out_shape=tuple(jax.ShapeDtypeStruct(s, d) for s, d in outs),
        in_specs=list(in_specs),
        out_specs=tuple(out_specs),
        scratch_shapes=list(scratch),
        name=kernel.__name__,
    )


def swap(axis, even, odd):
    count = lax.axis_size(axis)
    first = [(i, i ^ 1) for i in range(count) if i ^ 1 < count]
    second = []
    for i in range(1, count - 1, 2):
        second += [(i, i + 1), (i + 1, i)]
    return lax.ppermute(even, axis, first), lax.ppermute(odd, axis, second)


def matrices():
    weights = gauss_weights()
    size = 3 * LANES
    g = np.zeros((size, 2 * LANES), np.float32)
    band = np.zeros((size, size), np.float32)
    for col in range(size):
        for tap in range(-GAUSS_RADIUS, GAUSS_RADIUS + 1):
            if col < 2 * LANES:
                g[(col + tap) % size, col] = weights[tap + GAUSS_RADIUS]
            if abs(tap) <= BOX_RADIUS:
                band[(col + tap) % size, col] = 1.0
    hi, lo = split(jnp.asarray(g))
    return hi, lo, jnp.asarray(band).astype(BF16)


def on_device(moving_image, fixed_image, velocity, offsets, tissue):
    ix, iy = lax.axis_index("gx"), lax.axis_index("gy")
    ny = lax.axis_size("gy")
    table = jnp.concatenate(
        [
            jnp.stack([ix & 1, iy & 1, (iy > 0).astype(jnp.int32), (iy < ny - 1).astype(jnp.int32)]),
            offsets.reshape(12),
            tissue.reshape(4),
        ]
    ).astype(jnp.int32)
    rows = DEPTH * ROWS
    m = moving_image.reshape(rows, 2 * LANES)
    f = fixed_image.reshape(rows, 2 * LANES)
    v = velocity.reshape(3, rows, 2 * LANES)

    V, S, A = VMEM_SPEC, SMEM_SPEC, ANY_SPEC
    edge = ((272, 2 * LANES), BF16)
    xe, xo = call(edge_x_kernel, [edge, edge], [S, V, V], [V, V])(table, m, f)
    rxe, rxo = swap("gx", xe, xo)
    edge = ((384, LANES), BF16)
    ve, vo = call(edge_v_kernel, [edge, edge], [S, V], [V, V])(table, v)
    edge = ((Y_ROWS, LANES), BF16)
    ye, yo = call(edge_y_kernel, [edge, edge], [S] + [V] * 6, [V, V])(table, m, f, rxe, rxo, ve, vo)
    rye, ryo = swap("gy", ye, yo)

    edge = ((8, DEPTH, 3 * LANES), BF16)
    w, slope, we, wo = call(
        warp_kernel,
        [((ROWS, DEPTH, 3 * LANES), BF16), ((3, ROWS, DEPTH, 3 * LANES), F32), edge, edge],
        [S] + [V] * 5 + [A],
        [V] * 4,
        [
            pltpu.VMEM((3, 22 * EXT, LANES), F32),
            pltpu.VMEM((3, 3, rows, LANES), F32),
            pltpu.VMEM((2, 2, BX + 1, DEPTH, LANES), F32),
            pltpu.SemaphoreType.DMA((6,)),
        ],
    )(table, m, rxe, rxo, rye, ryo, v)
    rwe, rwo = swap("gx", we, wo)

    gh, gl, band = matrices()
    rows3 = (3, 3, rows, LANES)
    fx, sums, mask, own = call(
        window_kernel,
        [
            ((EXT, DEPTH, 3 * LANES), BF16),
            ((2, 3, DEPTH * OUT, LANES), F32),
            ((3, OUT, LANES), F32),
            (rows3, F32),
        ],
        [S] + [V] * 7,
        [V] * 4,
        [pltpu.VMEM((3, DEPTH * EXT, LANES), F32), pltpu.VMEM((2, 3, DEPTH * EXT, LANES), F32)],
    )(table, f, rxe, rxo, rye, ryo, w, band)

    edge = ((3, GAUSS_RADIUS, DEPTH, 2 * LANES), BF16)
    ys, ge, go, loss = call(
        gradient_kernel,
        [((3, ROWS, DEPTH, 2 * LANES), F32), edge, edge, ((DEPTH, LANES), F32)],
        [S] + [V] * 11,
        [V] * 4,
        [
            pltpu.VMEM((3, 3, 256, LANES), F32),
            pltpu.VMEM((3, 3, DEPTH * OUT, LANES), F32),
            pltpu.VMEM((3, 3, DEPTH * OUT, LANES), F32),
            pltpu.VMEM((3, 2, ROWS, DEPTH, 3 * LANES), BF16),
        ],
    )(table, w, rwe, rwo, fx, sums, mask, own, slope, band, gh, gl)
    rge, rgo = swap("gx", ge, go)

    devices = lax.axis_size("gx") * ny
    local = jnp.stack([jnp.sum(loss), jnp.sum(tissue).astype(F32)])
    line = jnp.pad(local, (0, LANES - 2)).reshape(1, 1, LANES)
    everyone = lax.all_to_all(jnp.broadcast_to(line, (devices, 1, LANES)), ("gx", "gy"), 0, 0)
    totals = jnp.sum(everyone, axis=(0, 1))
    similarity_loss = -totals[0] / (totals[1] * float(BX * BY * DEPTH))

    (update,) = call(
        smooth_kernel,
        [((3, rows, 2 * LANES), F32)],
        [S] + [V] * 3,
        [A],
        [
            pltpu.VMEM((2, 3, GAUSS_RADIUS, DEPTH, 2 * LANES), F32),
            pltpu.VMEM((rows, LANES), F32),
            pltpu.VMEM((3, 2, rows, LANES), F32),
            pltpu.SemaphoreType.DMA((6,)),
        ],
    )(table, ys, rge, rgo)
    return update.reshape(velocity.shape), similarity_loss


def solution(mesh):
    in_specs = (
        P(None, "gx", "gy"),
        P(None, "gx", "gy"),
        P(None, None, "gx", "gy"),
        P(None, "gx", "gy"),
        P("gx", "gy"),
    )
    out_specs = (P(None, None, "gx", "gy"), P())
    return jax.shard_map(
        on_device, mesh=mesh, in_specs=in_specs, out_specs=out_specs, check_vma=False
    )
```

```python
import math

import jax
import jax.numpy as jnp
import numpy as np
from jax import lax
from jax.experimental import pallas as pl
from jax.experimental.pallas import tpu as pltpu
from jax.sharding import PartitionSpec as P


DEPTH = 16
BX = 16
BY = 128
ROWS = 32
EXT = 48
OUT = 40
LANES = 128
GAUSS_RADIUS = 7
BOX_RADIUS = 4
GAUSS_SIGMA = 3.0
WINDOW_COUNT = 729.0
VAR_EPSILON = 1e-05
STEP_RATE = 16.0
F32 = jnp.float32
BF16 = jnp.bfloat16

VMEM_LIMIT = 28 << 20
VMEM_SPEC = pl.BlockSpec(memory_space=pltpu.VMEM)
SMEM_SPEC = pl.BlockSpec(memory_space=pltpu.SMEM)
ANY_SPEC = pl.BlockSpec(memory_space=pltpu.HBM)


def gauss_weights():
    raw = [
        math.exp(-float(tap * tap) / (2.0 * GAUSS_SIGMA * GAUSS_SIGMA))
        for tap in range(-GAUSS_RADIUS, GAUSS_RADIUS + 1)
    ]
    total = sum(raw)
    return [w / total for w in raw]


def unrolled(count):
    def run(body):
        for i in range(count):
            body(i)

    return run


def lane_iota(shape):
    return lax.broadcasted_iota(jnp.int32, shape, len(shape) - 1)


def roll(x, shift):
    shift = shift % LANES
    return x if shift == 0 else pltpu.roll(x, shift, len(x.shape) - 1)


def pack_edge(tile, groups, last):
    rows = tile.shape[0] // groups
    width = LANES // groups
    lane = lane_iota((rows, LANES))
    acc = None
    for k in range(groups):
        piece = roll(tile[k * rows : (k + 1) * rows], width * (k + 1) if last else width * k)
        acc = piece if acc is None else jnp.where(lane // width == k, piece, acc)
    return acc


def unpack_group(right, left, k, groups):
    width = LANES // groups
    r = roll(right, -width * k)
    l = roll(left, -width * (k + 1))
    return jnp.where(lane_iota(r.shape) < LANES // 2, r, l)


def pick(flag, a, b):
    return jnp.where(flag == 0, a, b)


def planes(x, rows):
    return x.reshape(DEPTH, rows, x.shape[-1])


def edge_x_kernel(t_hbm, m_hbm, f_hbm, e_ref, o_ref, t_scr, m_scr, f_scr, sem):
    copies = [
        pltpu.make_async_copy(src, dst, sem.at[i])
        for i, (src, dst) in enumerate(((m_hbm, m_scr), (f_hbm, f_scr), (t_hbm, t_scr)))
    ]
    for copy in copies:
        copy.start()
    px = lax.axis_index("gx") & 1
    lane = lane_iota((16, 2 * LANES))
    for n, ref in enumerate((m_scr, f_scr)):
        copies[n].wait()
        v = planes(ref[...].astype(F32), ROWS)
        first = v[:, :8].reshape(128, 2 * LANES)
        last = v[:, 24:].reshape(128, 2 * LANES)
        e_ref[128 * n : 128 * n + 128] = pick(px, last, first).astype(BF16)
        o_ref[128 * n : 128 * n + 128] = pick(px, first, last).astype(BF16)
    copies[2].wait()
    t = [[t_scr[i, j].astype(F32) for j in range(2)] for i in range(2)]
    first = jnp.where(lane < LANES, t[0][0], t[0][1])
    last = jnp.where(lane < LANES, t[1][0], t[1][1])
    e_ref[256:272] = pick(px, last, first).astype(BF16)
    o_ref[256:272] = pick(px, first, last).astype(BF16)


def edge_v_kernel(v_ref, e_ref, o_ref):
    py = lax.axis_index("gy") & 1
    for c in range(3):
        first = pack_edge(v_ref[c, :, :LANES], 8, False)
        last = pack_edge(v_ref[c, :, LANES:], 8, True)
        for ref, val in ((e_ref, pick(py, last, first)), (o_ref, pick(py, first, last))):
            hi = val.astype(BF16)
            ref[128 * c : 128 * c + 64] = hi
            ref[128 * c + 64 : 128 * c + 128] = (val - hi.astype(F32)).astype(BF16)


def before_after(px, e, o):
    return pick(px, o, e), pick(px, e, o)


def extended(own, e_ref, o_ref, px, base):
    e = e_ref[base : base + 128].astype(F32)
    o = o_ref[base : base + 128].astype(F32)
    before, after = before_after(px, e, o)
    return jnp.concatenate(
        [planes(before, 8), planes(own.astype(F32), ROWS), planes(after, 8)], axis=1
    )


def edge_y_kernel(off_ref, t_ref, m_ref, f_ref, xe_ref, xo_ref, ve_ref, vo_ref, e_ref, o_ref):
    px = lax.axis_index("gx") & 1
    py = lax.axis_index("gy") & 1
    row = 0
    for n, (ref, groups) in enumerate(((m_ref, 4), (f_ref, 8))):
        ext = extended(ref[...], xe_ref, xo_ref, px, 128 * n).reshape(DEPTH * EXT, 2 * LANES)
        first = pack_edge(ext[:, :LANES], groups, False)
        last = pack_edge(ext[:, LANES:], groups, True)
        size = first.shape[0]
        e_ref[row : row + size] = pick(py, last, first).astype(BF16)
        o_ref[row : row + size] = pick(py, first, last).astype(BF16)
        row += size
    e_ref[row : row + 384] = ve_ref[...]
    o_ref[row : row + 384] = vo_ref[...]
    row += 384
    before, after = before_after(px, xe_ref[256:272].astype(F32), xo_ref[256:272].astype(F32))
    lane = lane_iota((16, LANES))
    sides = []
    for j in range(2):
        acc = jnp.zeros((16, LANES), F32)
        for c in range(3):
            for i in range(2):
                acc = jnp.where(lane == 2 * c + i, off_ref[c, i, j].astype(F32), acc)
        tissue = (
            before[:, LANES * j : LANES * j + LANES],
            t_ref[0, j].astype(F32),
            t_ref[1, j].astype(F32),
            after[:, LANES * j : LANES * j + LANES],
        )
        for i, t in enumerate(tissue):
            acc = jnp.where(lane == 8 + i, t, acc)
        sides.append(acc)
    e_ref[row : row + 16] = pick(py, sides[1], sides[0]).astype(BF16)
    o_ref[row : row + 16] = pick(py, sides[0], sides[1]).astype(BF16)


Y_FIXED, Y_VEL, Y_META, Y_ROWS = 192, 288, 672, 688


def sides_of(py, e_ref, o_ref, start, size):
    e = e_ref[start : start + size].astype(F32)
    o = o_ref[start : start + size].astype(F32)
    left, right = before_after(py, e, o)
    return right, left


def warp_kernel(
    off_ref, m_ref, xe_ref, xo_ref, ye_ref, yo_ref, v_hbm,
    w_ref, slope_ref, e_ref, o_ref,
    m_scr, v_scr, r_scr, sem,
):
    px = lax.axis_index("gx") & 1
    py = lax.axis_index("gy") & 1
    copies = []
    for c in range(3):
        for j in range(2):
            copies.append(
                pltpu.make_async_copy(
                    v_hbm.at[c, :, pl.ds(LANES * j, LANES)], v_scr.at[c, j], sem.at[2 * c + j]
                )
            )
    for copy in copies:
        copy.start()

    zero = jnp.zeros((3 * EXT, LANES), F32)
    for j in range(3):
        m_scr[j, 0 : 3 * EXT] = zero
        m_scr[j, 19 * EXT : 22 * EXT] = zero
    ext = extended(m_ref[...], xe_ref, xo_ref, px, 0).reshape(DEPTH * EXT, 2 * LANES)
    m_scr[0, 3 * EXT : 19 * EXT] = ext[:, :LANES]
    m_scr[1, 3 * EXT : 19 * EXT] = ext[:, LANES:]
    right, left = sides_of(py, ye_ref, yo_ref, 0, 192)
    for k in range(4):
        m_scr[2, 3 * EXT + 192 * k : 3 * EXT + 192 * k + 192] = unpack_group(right, left, k, 4)
    for c in range(3):
        right, left = sides_of(py, ye_ref, yo_ref, Y_VEL + 128 * c, 128)
        right = right[:64] + right[64:]
        left = left[:64] + left[64:]
        for k in range(8):
            v_scr[c, 2, 64 * k : 64 * k + 64] = unpack_group(right, left, k, 8)
    digit = lax.broadcasted_iota(jnp.int32, (16, LANES), 1)
    power = (1 << (4 * jnp.minimum(digit, 5))).astype(F32)
    use = (lax.broadcasted_iota(jnp.int32, (16, LANES), 0) == 0) & (digit < 6)

    def offsets_of(meta):
        code = jnp.sum(jnp.where(use, (meta + 8.0) * power, 0.0)).astype(jnp.int32)
        return [((code >> (4 * k)) & 15) - 8 for k in range(6)]

    m_right, m_left = (offsets_of(x) for x in sides_of(py, ye_ref, yo_ref, Y_META, 16))
    lane = lane_iota((DEPTH, LANES))

    def gather(j, xb, oz, ox, oy, merge):
        shifts = []
        for b in range(2):
            s = oy + b
            nbr = jnp.where(s >= 0, (j + 1) % 3, (j + 2) % 3)
            lo = jnp.where(s >= 0, 0, LANES + s)
            hi = jnp.where(s >= 0, s, LANES)
            mask = (lane >= lo) & (lane < hi)
            shifts.append((nbr, mask, (LANES - s) & (LANES - 1)))
        base = (3 + oz) * EXT + xb * BX + 8 + ox

        @unrolled(BX + 1)
        def _(x):
            for c in range(2):
                start = base + c * EXT + x
                own = m_scr[j, pl.ds(start, DEPTH, stride=EXT), :]
                for b in range(2):
                    nbr, mask, amount = shifts[b]
                    other = m_scr[nbr, pl.ds(start, DEPTH, stride=EXT), :]
                    val = pltpu.roll(jnp.where(mask, other, own), amount, 1)
                    if merge:
                        val = jnp.where(lane < LANES // 2, r_scr[b, c, x], val)
                    r_scr[b, c, x] = val

    def blend(j, xb):
        @pl.loop(0, BX, unroll=4)
        def _(x):
            row = xb * BX + x
            f0, f1, f2 = (v_scr[c, j, pl.ds(row, DEPTH, stride=ROWS), :] for c in range(3))
            mid, dx, dy = [], [], []
            for c in range(2):
                low, dif = [], []
                for a in range(2):
                    s0 = r_scr[0, c, x + a]
                    d = r_scr[1, c, x + a] - s0
                    dif.append(d)
                    low.append(s0 + f2 * d)
                step = low[1] - low[0]
                dx.append(step)
                mid.append(low[0] + f1 * step)
                dy.append(dif[0] + f1 * (dif[1] - dif[0]))
            dz = mid[1] - mid[0]
            lanes = slice(LANES * j, LANES * j + LANES)
            w_ref[row, :, lanes] = (mid[0] + f0 * dz).astype(BF16)
            slope_ref[0, row, :, lanes] = dz
            slope_ref[1, row, :, lanes] = dx[0] + f0 * (dx[1] - dx[0])
            slope_ref[2, row, :, lanes] = dy[0] + f0 * (dy[1] - dy[0])

    for xb in range(2):
        gather(2, xb, *(m_right[2 * c + xb] for c in range(3)), False)
        gather(2, xb, *(m_left[2 * c + xb] for c in range(3)), True)
        blend(2, xb)
    for copy in copies:
        copy.wait()
    for j in range(2):
        for xb in range(2):
            gather(j, xb, *(off_ref[c, xb, j] for c in range(3)), False)
            blend(j, xb)
    e_ref[...] = w_ref[pl.ds(jnp.where(px == 0, ROWS - 8, 0), 8)]
    o_ref[...] = w_ref[pl.ds(jnp.where(px == 0, 0, ROWS - 8), 8)]


def box_x(load, store, count):
    v, three = {}, {}
    for x in range(count + 8):
        v[x] = load(x)
        if x >= 2:
            three[x - 2] = v[x - 2] + v[x - 1] + v[x]
        if x >= 8:
            store(x - 8, three[x - 8] + three[x - 5] + three[x - 2])


def add_all(terms):
    terms = [t for t in terms if t is not None]
    if not terms:
        return None
    total = terms[0]
    for t in terms[1:]:
        total = total + t
    return total


def box_column(v):
    three = {z: add_all([v[i] for i in (z - 1, z, z + 1) if 0 <= i < DEPTH]) for z in range(-3, 19)}
    return [add_all([three[z - 3], three[z], three[z + 3]]) for z in range(DEPTH)]


def split(v):
    hi = v.astype(BF16)
    return hi, (v - hi.astype(F32)).astype(BF16)


def dot(a, b):
    return jnp.dot(a, b, preferred_element_type=F32)


def box_y(parts, band):
    total = None
    for p in parts:
        d = dot(p, band)
        total = d if total is None else total + d
    return total


def put_tiles(ref, q, first, v):
    for j in range(3):
        ref[q, j, pl.ds(first, v.shape[0]), :] = v[:, LANES * j : LANES * j + LANES]


def box_z(src, dst, q, count):
    @pl.loop(0, count // 8)
    def _(t):
        for j in range(3):
            rows = [pl.ds(t * 128 + z, 8, stride=DEPTH) for z in range(DEPTH)]
            v = box_column([src[q, j, r, :] for r in rows])
            for z in range(DEPTH):
                dst[q, j, rows[z], :] = v[z]


def window_kernel(
    t_ref, f_ref, xe_ref, xo_ref, ye_ref, yo_ref, w_ref, band_ref,
    fx_ref, sum_ref, mask_ref, own_ref,
    f_scr, y_scr,
):
    px = lax.axis_index("gx") & 1
    py = lax.axis_index("gy") & 1
    ext = extended(f_ref[...], xe_ref, xo_ref, px, 128).reshape(DEPTH * EXT, 2 * LANES)
    f_scr[0] = ext[:, :LANES]
    f_scr[1] = ext[:, LANES:]
    right, left = sides_of(py, ye_ref, yo_ref, Y_FIXED, 96)
    for k in range(8):
        f_scr[2, 96 * k : 96 * k + 96] = unpack_group(right, left, k, 8)

    before, after = before_after(px, xe_ref[256:264].astype(F32), xo_ref[256:264].astype(F32))
    m_right, m_left = sides_of(py, ye_ref, yo_ref, Y_META, 8)
    row = lax.broadcasted_iota(jnp.int32, (OUT, LANES), 0)
    lane = lane_iota((8, LANES))

    def column(meta, k):
        picked = jnp.sum(jnp.where(lane == 8 + k, meta, 0.0), axis=1, keepdims=True)[:1]
        return jnp.broadcast_to(picked, (1, LANES))

    for j in range(3):
        if j < 2:
            lanes = slice(LANES * j, LANES * j + LANES)
            t = [
                before[:1, lanes],
                jnp.full((1, LANES), t_ref[0, j].astype(F32)),
                jnp.full((1, LANES), t_ref[1, j].astype(F32)),
                after[:1, lanes],
            ]
        else:
            half = lane_iota((1, LANES)) < LANES // 2
            t = [jnp.where(half, column(m_right, k), column(m_left, k)) for k in range(4)]
        mask_ref[j] = jnp.where(row < 4, t[0], jnp.where(row < 20, t[1], jnp.where(row < 36, t[2], t[3])))

    for x in range(EXT):
        for j in range(3):
            v = f_scr[j, pl.ds(x, DEPTH, stride=EXT), :]
            fx_ref[x, :, LANES * j : LANES * j + LANES] = v.astype(BF16)

    band = band_ref[...]
    for part in range(3):
        x = 16 * part
        f = fx_ref[x : x + 16].reshape(256, 3 * LANES)
        v = f.astype(F32)
        put_tiles(y_scr, 0, 256 * part, box_y([f], band))
        put_tiles(y_scr, 1, 256 * part, box_y(split(v * v), band))
    for part in range(2):
        x = 16 * part
        w = w_ref[x : x + 16].reshape(256, 3 * LANES)
        f = fx_ref[x + 8 : x + 24].reshape(256, 3 * LANES)
        image_sums(own_ref, 256 * part, w, f, band)
    for q in range(2):
        box_z(y_scr, y_scr, q, EXT)
        for j in range(3):
            def load(x):
                return y_scr[q, j, DEPTH * x : DEPTH * x + DEPTH]

            def store(x, v):
                sum_ref[q, j, DEPTH * x : DEPTH * x + DEPTH] = v

            box_x(load, store, OUT)
    for q in range(3):
        box_z(own_ref, own_ref, q, ROWS)


def image_sums(ref, first, w, f, band):
    i = w.astype(F32)
    put_tiles(ref, 0, first, box_y([w], band))
    put_tiles(ref, 1, first, box_y(split(i * i), band))
    put_tiles(ref, 2, first, box_y(split(i * f.astype(F32)), band))


def stats_kernel(
    t_ref, we_ref, wo_ref, fx_ref, sum_ref, mask_ref, own_ref, band_ref,
    a_ref, share_ref,
    h_scr, s_scr, n_scr,
):
    px = lax.axis_index("gx") & 1
    band = band_ref[...]
    before, after = before_after(px, we_ref[...].astype(F32), wo_ref[...].astype(F32))
    w = jnp.concatenate([before, after], axis=0).astype(BF16).reshape(256, 3 * LANES)
    f = jnp.concatenate([fx_ref[0:8], fx_ref[40:48]], axis=0).reshape(256, 3 * LANES)
    image_sums(h_scr, 0, w, f, band)
    for q in range(3):
        box_z(h_scr, h_scr, q, 16)

    @pl.loop(0, 3)
    def _(j):
        for q in range(3):
            def load(x):
                if 8 <= x < 40:
                    return own_ref[q, j, DEPTH * (x - 8) : DEPTH * (x - 7)]
                x = x if x < 8 else x - 32
                return h_scr[q, j, DEPTH * x : DEPTH * x + DEPTH]

            def store(x, v):
                s_scr[q, j, DEPTH * x : DEPTH * x + DEPTH] = v

            box_x(load, store, OUT)

    lane = lane_iota((DEPTH, LANES))
    near = (lane < 11) | (lane >= LANES - 11)

    def stats(x, inner):
        total = None
        first = x * DEPTH
        rows = pl.ds(pl.multiple_of(first, DEPTH) if inner else first, DEPTH)
        for j in range(3):
            si, sii, sij = (s_scr[q, j, rows, :] for q in range(3))
            sj = sum_ref[0, j, rows, :]
            sjj = sum_ref[1, j, rows, :]
            m = jnp.broadcast_to(mask_ref[j, pl.ds(x, 1), :], (DEPTH, LANES))
            cross = sij - si * sj * (1.0 / WINDOW_COUNT)
            var_i = sii - si * si * (1.0 / WINDOW_COUNT)
            var_j = sjj - sj * sj * (1.0 / WINDOW_COUNT)
            quotient = cross / (var_i * var_j + VAR_EPSILON)
            second = quotient * quotient * var_j
            adjoint = (
                (2.0 / WINDOW_COUNT) * m * (quotient * sj - second * si),
                m * second,
                -2.0 * m * quotient,
            )
            for k in range(3):
                a_ref[k, j, rows, :] = adjoint[k] if j < 2 else jnp.where(near, adjoint[k], 0.0)
            if inner and j < 2:
                ncc = m * (cross * quotient)
                total = ncc if total is None else total + ncc
        if inner:
            n_scr[...] += total

    n_scr[...] = jnp.zeros((DEPTH, LANES), F32)

    @pl.loop(0, ROWS, unroll=2)
    def _(x):
        stats(x + 4, True)

    for x in (0, 1, 2, 3, 36, 37, 38, 39):
        stats(x, False)

    blocks = (t_ref[0, 0] + t_ref[0, 1] + t_ref[1, 0] + t_ref[1, 1]).astype(F32)
    column = lane_iota(share_ref.shape)
    share_ref[...] = jnp.where(column == 0, jnp.sum(n_scr[...]), jnp.where(column == 1, blocks, 0.0))


def gradient_kernel(
    a_ref, w_ref, fx_ref, slope_ref, band_ref, gh_ref, gl_ref,
    ys_ref, e_ref, o_ref,
    a_scr, b_scr,
):
    px = lax.axis_index("gx") & 1
    band = band_ref[...]
    for k in range(3):
        box_z(a_ref, a_scr, k, OUT)

    for j in range(3):
        lanes = slice(LANES * j, LANES * j + LANES)
        for k in range(3):
            def load(x):
                return a_scr[k, j, DEPTH * x : DEPTH * x + DEPTH]

            def store(x, v):
                hi, lo = split(v)
                b_scr[k, 0, x, :, lanes] = hi
                b_scr[k, 1, x, :, lanes] = lo

            box_x(load, store, ROWS)

    column = lane_iota((1, 3 * LANES))
    r_lim = jnp.where(lax.axis_index("gy") < lax.axis_size("gy") - 1, 2 * LANES + GAUSS_RADIUS, 2 * LANES)
    l_lim = jnp.where(lax.axis_index("gy") > 0, 3 * LANES - GAUSS_RADIUS, 3 * LANES)
    valid = (column < r_lim) | (column >= l_lim)
    gh = gh_ref[...]
    gl = gl_ref[...]
    for part in range(2):
        x = 16 * part

        def flat(v):
            return v.reshape(256, 3 * LANES)

        spread = [
            box_y([flat(b_scr[k, i, x : x + 16]) for i in range(2)], band) for k in range(3)
        ]
        i = flat(w_ref[x : x + 16]).astype(F32)
        t = flat(fx_ref[x + 8 : x + 24]).astype(F32)
        grad = spread[0] + 2.0 * i * spread[1] + t * spread[2]
        for c in range(3):
            g = jnp.where(valid, grad * flat(slope_ref[c, x : x + 16]), 0.0)
            hi, lo = split(g)
            ys = dot(hi, gh) + dot(lo, gh) + dot(hi, gl)
            ys_ref[c, x : x + 16] = ys.reshape(16, DEPTH, 2 * LANES)
    for c in range(3):
        first = ys_ref[c, :GAUSS_RADIUS]
        last = ys_ref[c, ROWS - GAUSS_RADIUS :]
        e_ref[c] = pick(px, last, first).astype(BF16)
        o_ref[c] = pick(px, first, last).astype(BF16)


def smooth_kernel(ys_ref, ge_ref, go_ref, all_ref, out_hbm, loss_ref, h_scr, z_scr, o_scr, sem):
    weights = gauss_weights()
    px = lax.axis_index("gx") & 1
    r = GAUSS_RADIUS
    for c in range(3):
        before, after = before_after(px, ge_ref[c].astype(F32), go_ref[c].astype(F32))
        h_scr[0, c] = before
        h_scr[1, c] = after
    copies = []
    for c in range(3):
        for j in range(2):
            lanes = slice(LANES * j, LANES * j + LANES)

            def load(x):
                if x < r:
                    return h_scr[0, c, x, :, lanes]
                if x < r + ROWS:
                    return ys_ref[c, x - r, :, lanes]
                return h_scr[1, c, x - r - ROWS, :, lanes]

            for x in range(ROWS):
                total = (-STEP_RATE * weights[r]) * load(x + r)
                for k in range(1, r + 1):
                    total = total + (-STEP_RATE * weights[r + k]) * (load(x + r - k) + load(x + r + k))
                z_scr[pl.ds(x, DEPTH, stride=ROWS), :] = total

            @pl.loop(0, ROWS // 8)
            def _(t):
                def at(z):
                    return pl.multiple_of(z * ROWS + t * 8, 8)

                v = [z_scr[pl.ds(at(z), 8), :] for z in range(DEPTH)]
                for z in range(DEPTH):
                    total = weights[r] * v[z]
                    for k in range(1, r + 1):
                        pair = add_all([v[i] for i in (z - k, z + k) if 0 <= i < DEPTH])
                        if pair is not None:
                            total = total + weights[r + k] * pair
                    o_scr[c, j, pl.ds(at(z), 8), :] = total

            copy = pltpu.make_async_copy(
                o_scr.at[c, j], out_hbm.at[c, :, pl.ds(LANES * j, LANES)], sem.at[2 * c + j]
            )
            copy.start()
            copies.append(copy)
    column = lane_iota(all_ref.shape)
    shares = all_ref[...]
    total = jnp.sum(jnp.where(column == 0, shares, 0.0))
    blocks = jnp.sum(jnp.where(column == 1, shares, 0.0))
    row = jnp.full((1, LANES), -total) / (jnp.full((1, LANES), blocks) * float(BX * BY * DEPTH))
    loss_ref[...] = row
    for copy in copies:
        copy.wait()


def call(kernel, outs, in_specs, out_specs, scratch=(), limit=VMEM_LIMIT):
    return pl.pallas_call(
        kernel,
        out_shape=tuple(jax.ShapeDtypeStruct(s, d) for s, d in outs),
        in_specs=list(in_specs),
        out_specs=tuple(out_specs),
        scratch_shapes=list(scratch),
        compiler_params=pltpu.CompilerParams(vmem_limit_bytes=limit),
    )


def swap(axis, even, odd):
    count = lax.axis_size(axis)
    first = [(i, i ^ 1) for i in range(count) if i ^ 1 < count]
    second = []
    for i in range(1, count - 1, 2):
        second += [(i, i + 1), (i + 1, i)]
    even = lax.ppermute(even, axis, first)
    odd = lax.ppermute(odd, axis, second)
    return even, odd


def matrices():
    weights = gauss_weights()
    size = 3 * LANES
    g = np.zeros((size, 2 * LANES), np.float32)
    band = np.zeros((size, size), np.float32)
    for col in range(size):
        for tap in range(-GAUSS_RADIUS, GAUSS_RADIUS + 1):
            if col < 2 * LANES:
                g[(col + tap) % size, col] = weights[tap + GAUSS_RADIUS]
            if abs(tap) <= BOX_RADIUS:
                band[(col + tap) % size, col] = 1.0
    hi, lo = split(jnp.asarray(g))
    return hi, lo, jnp.asarray(band).astype(BF16)


def step(moving_image, fixed_image, velocity, offsets, tissue):
    rows = DEPTH * ROWS
    m = moving_image.reshape(rows, 2 * LANES)
    f = fixed_image.reshape(rows, 2 * LANES)
    v = velocity.reshape(3, rows, 2 * LANES)

    V, S, A = VMEM_SPEC, SMEM_SPEC, ANY_SPEC
    edge = ((272, 2 * LANES), BF16)
    xe, xo = call(
        edge_x_kernel,
        [edge, edge],
        [A] * 3,
        [V] * 2,
        [
            pltpu.SMEM((2, 2), jnp.int32),
            pltpu.VMEM((rows, 2 * LANES), BF16),
            pltpu.VMEM((rows, 2 * LANES), BF16),
            pltpu.SemaphoreType.DMA((3,)),
        ],
        60 << 20,
    )(tissue, m, f)
    rxe, rxo = swap("gx", xe, xo)
    edge = ((384, LANES), BF16)
    ve, vo = call(edge_v_kernel, [edge, edge], [V], [V, V])(v)
    edge = ((Y_ROWS, LANES), BF16)
    ye, yo = call(edge_y_kernel, [edge, edge], [S, S] + [V] * 6, [V, V])(
        offsets, tissue, m, f, rxe, rxo, ve, vo
    )
    rye, ryo = swap("gy", ye, yo)

    edge = ((8, DEPTH, 3 * LANES), BF16)
    w, slope, we, wo = call(
        warp_kernel,
        [((ROWS, DEPTH, 3 * LANES), BF16), ((3, ROWS, DEPTH, 3 * LANES), F32), edge, edge],
        [S] + [V] * 5 + [A],
        [V] * 4,
        [
            pltpu.VMEM((3, 22 * EXT, LANES), F32),
            pltpu.VMEM((3, 3, rows, LANES), F32),
            pltpu.VMEM((2, 2, BX + 1, DEPTH, LANES), F32),
            pltpu.SemaphoreType.DMA((6,)),
        ],
    )(offsets, m, rxe, rxo, rye, ryo, v)
    rwe, rwo = swap("gx", we, wo)

    gh, gl, band = matrices()
    rows3 = (3, 3, rows, LANES)
    fx, sums, mask, own = call(
        window_kernel,
        [
            ((EXT, DEPTH, 3 * LANES), BF16),
            ((2, 3, DEPTH * OUT, LANES), F32),
            ((3, OUT, LANES), F32),
            (rows3, F32),
        ],
        [S] + [V] * 7,
        [V] * 4,
        [pltpu.VMEM((3, DEPTH * EXT, LANES), F32), pltpu.VMEM((2, 3, DEPTH * EXT, LANES), F32)],
    )(tissue, f, rxe, rxo, rye, ryo, w, band)

    adjoint = ((3, 3, DEPTH * OUT, LANES), F32)
    adj, share = call(
        stats_kernel,
        [adjoint, ((8, LANES), F32)],
        [S] + [V] * 7,
        [V] * 2,
        [
            pltpu.VMEM((3, 3, 256, LANES), F32),
            pltpu.VMEM(*adjoint),
            pltpu.VMEM((DEPTH, LANES), F32),
        ],
    )(tissue, rwe, rwo, fx, sums, mask, own, band)

    edge = ((3, GAUSS_RADIUS, DEPTH, 2 * LANES), BF16)
    ys, ge, go = call(
        gradient_kernel,
        [((3, ROWS, DEPTH, 2 * LANES), F32), edge, edge],
        [V] * 7,
        [V] * 3,
        [pltpu.VMEM(*adjoint), pltpu.VMEM((3, 2, ROWS, DEPTH, 3 * LANES), BF16)],
    )(adj, w, fx, slope, band, gh, gl)
    rge, rgo = swap("gx", ge, go)

    nx, ny = lax.axis_size("gx"), lax.axis_size("gy")
    other = lax.ppermute(share, "gy", [(i, i ^ 1) for i in range(ny)])
    line = (share[:1] + other[:1]).reshape(1, 1, LANES)
    groups = [[i * ny + j for i in range(nx) for j in range(p, ny, 2)] for p in range(2)]
    count = nx * ny // 2
    everyone = lax.all_to_all(
        jnp.broadcast_to(line, (count, 1, LANES)), ("gx", "gy"), 0, 0, axis_index_groups=groups
    )
    everyone = everyone.reshape(count, LANES)

    update, loss = call(
        smooth_kernel,
        [((3, rows, 2 * LANES), F32), ((1, LANES), F32)],
        [V] * 4,
        [A, V],
        [
            pltpu.VMEM((2, 3, GAUSS_RADIUS, DEPTH, 2 * LANES), F32),
            pltpu.VMEM((rows, LANES), F32),
            pltpu.VMEM((3, 2, rows, LANES), F32),
            pltpu.SemaphoreType.DMA((6,)),
        ],
    )(ys, rge, rgo, everyone)
    return update.reshape(velocity.shape), loss[0, 0]


def solution(mesh):
    in_specs = (
        P(None, "gx", "gy"),
        P(None, "gx", "gy"),
        P(None, None, "gx", "gy"),
        P(None, "gx", "gy"),
        P("gx", "gy"),
    )
    out_specs = (P(None, None, "gx", "gy"), P())
    return jax.shard_map(step, mesh=mesh, in_specs=in_specs, out_specs=out_specs, check_vma=False)
```

```python
import math

import jax
import jax.numpy as jnp
import numpy as np
from jax import lax
from jax.experimental import pallas as pl
from jax.experimental.pallas import tpu as pltpu
from jax.sharding import PartitionSpec as P


DEPTH = 16
BX = 16
BY = 128
ROWS = 32
EXT = 48
OUT = 40
LANES = 128
GAUSS_RADIUS = 7
BOX_RADIUS = 4
GAUSS_SIGMA = 3.0
WINDOW_COUNT = 729.0
VAR_EPSILON = 1e-05
STEP_RATE = 16.0
F32 = jnp.float32
BF16 = jnp.bfloat16

VMEM_LIMIT = 28 << 20
VMEM_SPEC = pl.BlockSpec(memory_space=pltpu.VMEM)
SMEM_SPEC = pl.BlockSpec(memory_space=pltpu.SMEM)
ANY_SPEC = pl.BlockSpec(memory_space=pltpu.HBM)


def gauss_weights():
    raw = [
        math.exp(-float(tap * tap) / (2.0 * GAUSS_SIGMA * GAUSS_SIGMA))
        for tap in range(-GAUSS_RADIUS, GAUSS_RADIUS + 1)
    ]
    total = sum(raw)
    return [w / total for w in raw]


def unrolled(count):
    def run(body):
        for i in range(count):
            body(i)

    return run


def lane_iota(shape):
    return lax.broadcasted_iota(jnp.int32, shape, len(shape) - 1)


def roll(x, shift):
    shift = shift % LANES
    return x if shift == 0 else pltpu.roll(x, shift, len(x.shape) - 1)


def pack_edge(tile, groups, last):
    rows = tile.shape[0] // groups
    width = LANES // groups
    lane = lane_iota((rows, LANES))
    acc = None
    for k in range(groups):
        piece = roll(tile[k * rows : (k + 1) * rows], width * (k + 1) if last else width * k)
        acc = piece if acc is None else jnp.where(lane // width == k, piece, acc)
    return acc


def unpack_group(right, left, k, groups):
    width = LANES // groups
    r = roll(right, -width * k)
    l = roll(left, -width * (k + 1))
    return jnp.where(lane_iota(r.shape) < LANES // 2, r, l)


def pick(flag, a, b):
    return jnp.where(flag == 0, a, b)


def planes(x, rows):
    return x.reshape(DEPTH, rows, x.shape[-1])


def edge_x_kernel(t_hbm, m_hbm, f_hbm, e_ref, o_ref, t_scr, m_scr, f_scr, sem):
    copies = [
        pltpu.make_async_copy(src, dst, sem.at[i])
        for i, (src, dst) in enumerate(((m_hbm, m_scr), (f_hbm, f_scr), (t_hbm, t_scr)))
    ]
    for copy in copies:
        copy.start()
    px = lax.axis_index("gx") & 1
    lane = lane_iota((16, 2 * LANES))
    for n, ref in enumerate((m_scr, f_scr)):
        copies[n].wait()
        v = planes(ref[...].astype(F32), ROWS)
        first = v[:, :8].reshape(128, 2 * LANES)
        last = v[:, 24:].reshape(128, 2 * LANES)
        e_ref[128 * n : 128 * n + 128] = pick(px, last, first).astype(BF16)
        o_ref[128 * n : 128 * n + 128] = pick(px, first, last).astype(BF16)
    copies[2].wait()
    t = [[t_scr[i, j].astype(F32) for j in range(2)] for i in range(2)]
    first = jnp.where(lane < LANES, t[0][0], t[0][1])
    last = jnp.where(lane < LANES, t[1][0], t[1][1])
    e_ref[256:272] = pick(px, last, first).astype(BF16)
    o_ref[256:272] = pick(px, first, last).astype(BF16)


def edge_v_kernel(v_ref, e_ref, o_ref):
    py = lax.axis_index("gy") & 1
    for c in range(3):
        first = pack_edge(v_ref[c, :, :LANES], 8, False)
        last = pack_edge(v_ref[c, :, LANES:], 8, True)
        for ref, val in ((e_ref, pick(py, last, first)), (o_ref, pick(py, first, last))):
            hi = val.astype(BF16)
            ref[128 * c : 128 * c + 64] = hi
            ref[128 * c + 64 : 128 * c + 128] = (val - hi.astype(F32)).astype(BF16)


def before_after(px, e, o):
    return pick(px, o, e), pick(px, e, o)


def extended(own, e_ref, o_ref, px, base):
    e = e_ref[base : base + 128].astype(F32)
    o = o_ref[base : base + 128].astype(F32)
    before, after = before_after(px, e, o)
    return jnp.concatenate(
        [planes(before, 8), planes(own.astype(F32), ROWS), planes(after, 8)], axis=1
    )


def edge_y_kernel(off_ref, t_ref, m_ref, f_ref, xe_ref, xo_ref, ve_ref, vo_ref, e_ref, o_ref):
    px = lax.axis_index("gx") & 1
    py = lax.axis_index("gy") & 1
    row = 0
    for n, (ref, groups) in enumerate(((m_ref, 4), (f_ref, 8))):
        ext = extended(ref[...], xe_ref, xo_ref, px, 128 * n).reshape(DEPTH * EXT, 2 * LANES)
        first = pack_edge(ext[:, :LANES], groups, False)
        last = pack_edge(ext[:, LANES:], groups, True)
        size = first.shape[0]
        e_ref[row : row + size] = pick(py, last, first).astype(BF16)
        o_ref[row : row + size] = pick(py, first, last).astype(BF16)
        row += size
    e_ref[row : row + 384] = ve_ref[...]
    o_ref[row : row + 384] = vo_ref[...]
    row += 384
    before, after = before_after(px, xe_ref[256:272].astype(F32), xo_ref[256:272].astype(F32))
    lane = lane_iota((16, LANES))
    sides = []
    for j in range(2):
        acc = jnp.zeros((16, LANES), F32)
        for c in range(3):
            for i in range(2):
                acc = jnp.where(lane == 2 * c + i, off_ref[c, i, j].astype(F32), acc)
        tissue = (
            before[:, LANES * j : LANES * j + LANES],
            t_ref[0, j].astype(F32),
            t_ref[1, j].astype(F32),
            after[:, LANES * j : LANES * j + LANES],
        )
        for i, t in enumerate(tissue):
            acc = jnp.where(lane == 8 + i, t, acc)
        sides.append(acc)
    e_ref[row : row + 16] = pick(py, sides[1], sides[0]).astype(BF16)
    o_ref[row : row + 16] = pick(py, sides[0], sides[1]).astype(BF16)


Y_FIXED, Y_VEL, Y_META, Y_ROWS = 192, 288, 672, 688


def sides_of(py, e_ref, o_ref, start, size):
    e = e_ref[start : start + size].astype(F32)
    o = o_ref[start : start + size].astype(F32)
    left, right = before_after(py, e, o)
    return right, left


def warp_kernel(
    off_ref, m_ref, xe_ref, xo_ref, ye_ref, yo_ref, v_hbm,
    w_ref, slope_ref, e_ref, o_ref,
    m_scr, v_scr, r_scr, sem,
):
    px = lax.axis_index("gx") & 1
    py = lax.axis_index("gy") & 1
    copies = []
    for c in range(3):
        for j in range(2):
            copies.append(
                pltpu.make_async_copy(
                    v_hbm.at[c, :, pl.ds(LANES * j, LANES)], v_scr.at[c, j], sem.at[2 * c + j]
                )
            )
    for copy in copies:
        copy.start()

    zero = jnp.zeros((3 * EXT, LANES), F32)
    for j in range(3):
        m_scr[j, 0 : 3 * EXT] = zero
        m_scr[j, 19 * EXT : 22 * EXT] = zero
    ext = extended(m_ref[...], xe_ref, xo_ref, px, 0).reshape(DEPTH * EXT, 2 * LANES)
    m_scr[0, 3 * EXT : 19 * EXT] = ext[:, :LANES]
    m_scr[1, 3 * EXT : 19 * EXT] = ext[:, LANES:]
    right, left = sides_of(py, ye_ref, yo_ref, 0, 192)
    for k in range(4):
        m_scr[2, 3 * EXT + 192 * k : 3 * EXT + 192 * k + 192] = unpack_group(right, left, k, 4)
    for c in range(3):
        right, left = sides_of(py, ye_ref, yo_ref, Y_VEL + 128 * c, 128)
        right = right[:64] + right[64:]
        left = left[:64] + left[64:]
        for k in range(8):
            v_scr[c, 2, 64 * k : 64 * k + 64] = unpack_group(right, left, k, 8)
    digit = lax.broadcasted_iota(jnp.int32, (16, LANES), 1)
    power = (1 << (4 * jnp.minimum(digit, 5))).astype(F32)
    use = (lax.broadcasted_iota(jnp.int32, (16, LANES), 0) == 0) & (digit < 6)

    def offsets_of(meta):
        code = jnp.sum(jnp.where(use, (meta + 8.0) * power, 0.0)).astype(jnp.int32)
        return [((code >> (4 * k)) & 15) - 8 for k in range(6)]

    m_right, m_left = (offsets_of(x) for x in sides_of(py, ye_ref, yo_ref, Y_META, 16))
    lane = lane_iota((DEPTH, LANES))

    def gather(j, xb, oz, ox, oy, merge):
        nbr = jnp.where(oy >= 0, (j + 1) % 3, (j + 2) % 3)
        shifts = []
        for b in range(2):
            s = oy + b
            lo = jnp.where(s >= 0, 0, LANES + s)
            hi = jnp.where(s >= 0, s, LANES)
            mask = (lane >= lo) & (lane < hi)
            shifts.append((mask, (LANES - s) & (LANES - 1)))
        base = (3 + oz) * EXT + xb * BX + 8 + ox

        @unrolled(BX + 1)
        def _(x):
            for c in range(2):
                start = base + c * EXT + x
                own = m_scr[j, pl.ds(start, DEPTH, stride=EXT), :]
                other = m_scr[nbr, pl.ds(start, DEPTH, stride=EXT), :]
                for b in range(2):
                    mask, amount = shifts[b]
                    val = pltpu.roll(jnp.where(mask, other, own), amount, 1)
                    if merge:
                        val = jnp.where(lane < LANES // 2, r_scr[b, c, x], val)
                    r_scr[b, c, x] = val

    def blend(j, xb):
        @pl.loop(0, BX, unroll=8)
        def _(x):
            row = xb * BX + x
            f0, f1, f2 = (v_scr[c, j, pl.ds(row, DEPTH, stride=ROWS), :] for c in range(3))
            mid, dx, dy = [], [], []
            for c in range(2):
                low, dif = [], []
                for a in range(2):
                    s0 = r_scr[0, c, x + a]
                    d = r_scr[1, c, x + a] - s0
                    dif.append(d)
                    low.append(s0 + f2 * d)
                step = low[1] - low[0]
                dx.append(step)
                mid.append(low[0] + f1 * step)
                dy.append(dif[0] + f1 * (dif[1] - dif[0]))
            dz = mid[1] - mid[0]
            lanes = slice(LANES * j, LANES * j + LANES)
            w_ref[row, :, lanes] = (mid[0] + f0 * dz).astype(BF16)
            slope_ref[0, row, :, lanes] = dz
            slope_ref[1, row, :, lanes] = dx[0] + f0 * (dx[1] - dx[0])
            slope_ref[2, row, :, lanes] = dy[0] + f0 * (dy[1] - dy[0])

    for xb in range(2):
        gather(2, xb, *(m_right[2 * c + xb] for c in range(3)), False)
        gather(2, xb, *(m_left[2 * c + xb] for c in range(3)), True)
        blend(2, xb)
    for copy in copies:
        copy.wait()
    for j in range(2):
        for xb in range(2):
            gather(j, xb, *(off_ref[c, xb, j] for c in range(3)), False)
            blend(j, xb)
    e_ref[...] = w_ref[pl.ds(jnp.where(px == 0, ROWS - 8, 0), 8)]
    o_ref[...] = w_ref[pl.ds(jnp.where(px == 0, 0, ROWS - 8), 8)]


def box_x(load, store, count):
    v, three = {}, {}
    for x in range(count + 8):
        v[x] = load(x)
        if x >= 2:
            three[x - 2] = v[x - 2] + v[x - 1] + v[x]
        if x >= 8:
            store(x - 8, three[x - 8] + three[x - 5] + three[x - 2])


def add_all(terms):
    terms = [t for t in terms if t is not None]
    if not terms:
        return None
    total = terms[0]
    for t in terms[1:]:
        total = total + t
    return total


def box_column(v):
    three = {z: add_all([v[i] for i in (z - 1, z, z + 1) if 0 <= i < DEPTH]) for z in range(-3, 19)}
    return [add_all([three[z - 3], three[z], three[z + 3]]) for z in range(DEPTH)]


def split(v):
    hi = v.astype(BF16)
    return hi, (v - hi.astype(F32)).astype(BF16)


def dot(a, b):
    return jnp.dot(a, b, preferred_element_type=F32)


def box_y(parts, band):
    total = None
    for p in parts:
        d = dot(p, band)
        total = d if total is None else total + d
    return total


def put_tiles(ref, q, first, v):
    for j in range(3):
        ref[q, j, pl.ds(first, v.shape[0]), :] = v[:, LANES * j : LANES * j + LANES]


def box_z(src, dst, q, count):
    @unrolled(count // 8)
    def _(t):
        for j in range(3):
            rows = [pl.ds(t * 128 + z, 8, stride=DEPTH) for z in range(DEPTH)]
            v = box_column([src[q, j, r, :] for r in rows])
            for z in range(DEPTH):
                dst[q, j, rows[z], :] = v[z]


def window_kernel(
    t_ref, f_ref, xe_ref, xo_ref, ye_ref, yo_ref, w_ref, band_ref,
    fx_ref, sum_ref, mask_ref, own_ref,
    f_scr, y_scr,
):
    px = lax.axis_index("gx") & 1
    py = lax.axis_index("gy") & 1
    ext = extended(f_ref[...], xe_ref, xo_ref, px, 128).reshape(DEPTH * EXT, 2 * LANES)
    f_scr[0] = ext[:, :LANES]
    f_scr[1] = ext[:, LANES:]
    right, left = sides_of(py, ye_ref, yo_ref, Y_FIXED, 96)
    for k in range(8):
        f_scr[2, 96 * k : 96 * k + 96] = unpack_group(right, left, k, 8)

    before, after = before_after(px, xe_ref[256:264].astype(F32), xo_ref[256:264].astype(F32))
    m_right, m_left = sides_of(py, ye_ref, yo_ref, Y_META, 8)
    row = lax.broadcasted_iota(jnp.int32, (OUT, LANES), 0)
    lane = lane_iota((8, LANES))

    def column(meta, k):
        picked = jnp.sum(jnp.where(lane == 8 + k, meta, 0.0), axis=1, keepdims=True)[:1]
        return jnp.broadcast_to(picked, (1, LANES))

    for j in range(3):
        if j < 2:
            lanes = slice(LANES * j, LANES * j + LANES)
            t = [
                before[:1, lanes],
                jnp.full((1, LANES), t_ref[0, j].astype(F32)),
                jnp.full((1, LANES), t_ref[1, j].astype(F32)),
                after[:1, lanes],
            ]
        else:
            half = lane_iota((1, LANES)) < LANES // 2
            t = [jnp.where(half, column(m_right, k), column(m_left, k)) for k in range(4)]
        mask_ref[j] = jnp.where(row < 4, t[0], jnp.where(row < 20, t[1], jnp.where(row < 36, t[2], t[3])))

    for x in range(EXT):
        for j in range(3):
            v = f_scr[j, pl.ds(x, DEPTH, stride=EXT), :]
            fx_ref[x, :, LANES * j : LANES * j + LANES] = v.astype(BF16)

    band = band_ref[...]
    for part in range(3):
        x = 16 * part
        f = fx_ref[x : x + 16].reshape(256, 3 * LANES)
        v = f.astype(F32)
        put_tiles(y_scr, 0, 256 * part, box_y([f], band))
        put_tiles(y_scr, 1, 256 * part, box_y(split(v * v), band))
    for part in range(2):
        x = 16 * part
        w = w_ref[x : x + 16].reshape(256, 3 * LANES)
        f = fx_ref[x + 8 : x + 24].reshape(256, 3 * LANES)
        image_sums(own_ref, 256 * part, w, f, band)
    for q in range(2):
        box_z(y_scr, y_scr, q, EXT)
        for j in range(3):
            def load(x):
                return y_scr[q, j, DEPTH * x : DEPTH * x + DEPTH]

            def store(x, v):
                sum_ref[q, j, DEPTH * x : DEPTH * x + DEPTH] = v

            box_x(load, store, OUT)
    for q in range(3):
        box_z(own_ref, own_ref, q, ROWS)


def image_sums(ref, first, w, f, band):
    i = w.astype(F32)
    put_tiles(ref, 0, first, box_y([w], band))
    put_tiles(ref, 1, first, box_y(split(i * i), band))
    put_tiles(ref, 2, first, box_y(split(i * f.astype(F32)), band))


def stats_kernel(
    t_ref, we_ref, wo_ref, fx_ref, sum_ref, mask_ref, own_ref, band_ref,
    a_ref, share_ref,
    h_scr, s_scr, n_scr,
):
    px = lax.axis_index("gx") & 1
    band = band_ref[...]
    before, after = before_after(px, we_ref[...].astype(F32), wo_ref[...].astype(F32))
    w = jnp.concatenate([before, after], axis=0).astype(BF16).reshape(256, 3 * LANES)
    f = jnp.concatenate([fx_ref[0:8], fx_ref[40:48]], axis=0).reshape(256, 3 * LANES)
    image_sums(h_scr, 0, w, f, band)
    for q in range(3):
        box_z(h_scr, h_scr, q, 16)

    @pl.loop(0, 3)
    def _(j):
        for q in range(3):
            def load(x):
                if 8 <= x < 40:
                    return own_ref[q, j, DEPTH * (x - 8) : DEPTH * (x - 7)]
                x = x if x < 8 else x - 32
                return h_scr[q, j, DEPTH * x : DEPTH * x + DEPTH]

            def store(x, v):
                s_scr[q, j, DEPTH * x : DEPTH * x + DEPTH] = v

            box_x(load, store, OUT)

    lane = lane_iota((DEPTH, LANES))
    near = (lane < 11) | (lane >= LANES - 11)

    def stats(x, inner):
        total = None
        first = x * DEPTH
        rows = pl.ds(pl.multiple_of(first, DEPTH) if inner else first, DEPTH)
        for j in range(3):
            si, sii, sij = (s_scr[q, j, rows, :] for q in range(3))
            sj = sum_ref[0, j, rows, :]
            sjj = sum_ref[1, j, rows, :]
            m = jnp.broadcast_to(mask_ref[j, pl.ds(x, 1), :], (DEPTH, LANES))
            cross = sij - si * sj * (1.0 / WINDOW_COUNT)
            var_i = sii - si * si * (1.0 / WINDOW_COUNT)
            var_j = sjj - sj * sj * (1.0 / WINDOW_COUNT)
            quotient = cross / (var_i * var_j + VAR_EPSILON)
            second = quotient * quotient * var_j
            adjoint = (
                (2.0 / WINDOW_COUNT) * m * (quotient * sj - second * si),
                m * second,
                -2.0 * m * quotient,
            )
            for k in range(3):
                a_ref[k, j, rows, :] = adjoint[k] if j < 2 else jnp.where(near, adjoint[k], 0.0)
            if inner and j < 2:
                ncc = m * (cross * quotient)
                total = ncc if total is None else total + ncc
        if inner:
            n_scr[...] += total

    n_scr[...] = jnp.zeros((DEPTH, LANES), F32)

    @pl.loop(0, ROWS, unroll=2)
    def _(x):
        stats(x + 4, True)

    for x in (0, 1, 2, 3, 36, 37, 38, 39):
        stats(x, False)

    blocks = (t_ref[0, 0] + t_ref[0, 1] + t_ref[1, 0] + t_ref[1, 1]).astype(F32)
    column = lane_iota(share_ref.shape)
    share_ref[...] = jnp.where(column == 0, jnp.sum(n_scr[...]), jnp.where(column == 1, blocks, 0.0))


def gradient_kernel(
    a_ref, w_ref, fx_ref, slope_ref, band_ref, gh_ref, gl_ref,
    ys_ref, e_ref, o_ref,
    a_scr, b_scr,
):
    px = lax.axis_index("gx") & 1
    band = band_ref[...]
    for k in range(3):
        box_z(a_ref, a_scr, k, OUT)

    for j in range(3):
        lanes = slice(LANES * j, LANES * j + LANES)
        for k in range(3):
            def load(x):
                return a_scr[k, j, DEPTH * x : DEPTH * x + DEPTH]

            def store(x, v):
                hi, lo = split(v)
                b_scr[k, 0, x, :, lanes] = hi
                b_scr[k, 1, x, :, lanes] = lo

            box_x(load, store, ROWS)

    column = lane_iota((1, 3 * LANES))
    r_lim = jnp.where(lax.axis_index("gy") < lax.axis_size("gy") - 1, 2 * LANES + GAUSS_RADIUS, 2 * LANES)
    l_lim = jnp.where(lax.axis_index("gy") > 0, 3 * LANES - GAUSS_RADIUS, 3 * LANES)
    valid = (column < r_lim) | (column >= l_lim)
    gh = gh_ref[...]
    gl = gl_ref[...]
    for part in range(2):
        x = 16 * part

        def flat(v):
            return v.reshape(256, 3 * LANES)

        spread = [
            box_y([flat(b_scr[k, i, x : x + 16]) for i in range(2)], band) for k in range(3)
        ]
        i = flat(w_ref[x : x + 16]).astype(F32)
        t = flat(fx_ref[x + 8 : x + 24]).astype(F32)
        grad = spread[0] + 2.0 * i * spread[1] + t * spread[2]
        for c in range(3):
            g = jnp.where(valid, grad * flat(slope_ref[c, x : x + 16]), 0.0)
            hi, lo = split(g)
            ys = dot(hi, gh) + dot(lo, gh) + dot(hi, gl)
            ys_ref[c, x : x + 16] = ys.reshape(16, DEPTH, 2 * LANES)
    for c in range(3):
        first = ys_ref[c, :GAUSS_RADIUS]
        last = ys_ref[c, ROWS - GAUSS_RADIUS :]
        e_ref[c] = pick(px, last, first).astype(BF16)
        o_ref[c] = pick(px, first, last).astype(BF16)


def smooth_kernel(ys_ref, ge_ref, go_ref, out_hbm, h_scr, z_scr, o_scr, sem):
    weights = gauss_weights()
    px = lax.axis_index("gx") & 1
    r = GAUSS_RADIUS
    for c in range(3):
        before, after = before_after(px, ge_ref[c].astype(F32), go_ref[c].astype(F32))
        h_scr[0, c] = before
        h_scr[1, c] = after
    copies = []
    for c in range(3):
        for j in range(2):
            lanes = slice(LANES * j, LANES * j + LANES)

            def load(x):
                if x < r:
                    return h_scr[0, c, x, :, lanes]
                if x < r + ROWS:
                    return ys_ref[c, x - r, :, lanes]
                return h_scr[1, c, x - r - ROWS, :, lanes]

            for x in range(ROWS):
                total = (-STEP_RATE * weights[r]) * load(x + r)
                for k in range(1, r + 1):
                    total = total + (-STEP_RATE * weights[r + k]) * (load(x + r - k) + load(x + r + k))
                z_scr[pl.ds(x, DEPTH, stride=ROWS), :] = total

            @pl.loop(0, ROWS // 8)
            def _(t):
                def at(z):
                    return pl.multiple_of(z * ROWS + t * 8, 8)

                v = [z_scr[pl.ds(at(z), 8), :] for z in range(DEPTH)]
                for z in range(DEPTH):
                    total = weights[r] * v[z]
                    for k in range(1, r + 1):
                        pair = add_all([v[i] for i in (z - k, z + k) if 0 <= i < DEPTH])
                        if pair is not None:
                            total = total + weights[r + k] * pair
                    o_scr[c, j, pl.ds(at(z), 8), :] = total

            copy = pltpu.make_async_copy(
                o_scr.at[c, j], out_hbm.at[c, :, pl.ds(LANES * j, LANES)], sem.at[2 * c + j]
            )
            copy.start()
            copies.append(copy)
    for copy in copies:
        copy.wait()


def loss_kernel(all_ref, loss_ref):
    column = lane_iota(all_ref.shape)
    shares = all_ref[...]
    total = jnp.sum(jnp.where(column == 0, shares, 0.0))
    blocks = jnp.sum(jnp.where(column == 1, shares, 0.0))
    row = jnp.full((1, LANES), -total) / (jnp.full((1, LANES), blocks) * float(BX * BY * DEPTH))
    loss_ref[...] = row


def call(kernel, outs, in_specs, out_specs, scratch=(), limit=VMEM_LIMIT):
    return pl.pallas_call(
        kernel,
        out_shape=tuple(jax.ShapeDtypeStruct(s, d) for s, d in outs),
        in_specs=list(in_specs),
        out_specs=tuple(out_specs),
        scratch_shapes=list(scratch),
        compiler_params=pltpu.CompilerParams(vmem_limit_bytes=limit),
    )


def swap(axis, even, odd):
    count = lax.axis_size(axis)
    first = [(i, i ^ 1) for i in range(count) if i ^ 1 < count]
    second = []
    for i in range(1, count - 1, 2):
        second += [(i, i + 1), (i + 1, i)]
    even = lax.ppermute(even, axis, first)
    odd = lax.ppermute(odd, axis, second)
    return even, odd


def matrices():
    weights = gauss_weights()
    size = 3 * LANES
    g = np.zeros((size, 2 * LANES), np.float32)
    band = np.zeros((size, size), np.float32)
    for col in range(size):
        for tap in range(-GAUSS_RADIUS, GAUSS_RADIUS + 1):
            if col < 2 * LANES:
                g[(col + tap) % size, col] = weights[tap + GAUSS_RADIUS]
            if abs(tap) <= BOX_RADIUS:
                band[(col + tap) % size, col] = 1.0
    hi, lo = split(jnp.asarray(g))
    return hi, lo, jnp.asarray(band).astype(BF16)


def step(moving_image, fixed_image, velocity, offsets, tissue):
    rows = DEPTH * ROWS
    m = moving_image.reshape(rows, 2 * LANES)
    f = fixed_image.reshape(rows, 2 * LANES)
    v = velocity.reshape(3, rows, 2 * LANES)

    V, S, A = VMEM_SPEC, SMEM_SPEC, ANY_SPEC
    edge = ((272, 2 * LANES), BF16)
    xe, xo = call(
        edge_x_kernel,
        [edge, edge],
        [A] * 3,
        [V] * 2,
        [
            pltpu.SMEM((2, 2), jnp.int32),
            pltpu.VMEM((rows, 2 * LANES), BF16),
            pltpu.VMEM((rows, 2 * LANES), BF16),
            pltpu.SemaphoreType.DMA((3,)),
        ],
        60 << 20,
    )(tissue, m, f)
    rxe, rxo = swap("gx", xe, xo)
    edge = ((384, LANES), BF16)
    ve, vo = call(edge_v_kernel, [edge, edge], [V], [V, V])(v)
    edge = ((Y_ROWS, LANES), BF16)
    ye, yo = call(edge_y_kernel, [edge, edge], [S, S] + [V] * 6, [V, V])(
        offsets, tissue, m, f, rxe, rxo, ve, vo
    )
    rye, ryo = swap("gy", ye, yo)

    edge = ((8, DEPTH, 3 * LANES), BF16)
    w, slope, we, wo = call(
        warp_kernel,
        [((ROWS, DEPTH, 3 * LANES), BF16), ((3, ROWS, DEPTH, 3 * LANES), F32), edge, edge],
        [S] + [V] * 5 + [A],
        [V] * 4,
        [
            pltpu.VMEM((3, 22 * EXT, LANES), F32),
            pltpu.VMEM((3, 3, rows, LANES), F32),
            pltpu.VMEM((2, 2, BX + 1, DEPTH, LANES), F32),
            pltpu.SemaphoreType.DMA((6,)),
        ],
    )(offsets, m, rxe, rxo, rye, ryo, v)
    rwe, rwo = swap("gx", we, wo)

    gh, gl, band = matrices()
    rows3 = (3, 3, rows, LANES)
    fx, sums, mask, own = call(
        window_kernel,
        [
            ((EXT, DEPTH, 3 * LANES), BF16),
            ((2, 3, DEPTH * OUT, LANES), F32),
            ((3, OUT, LANES), F32),
            (rows3, F32),
        ],
        [S] + [V] * 7,
        [V] * 4,
        [pltpu.VMEM((3, DEPTH * EXT, LANES), F32), pltpu.VMEM((2, 3, DEPTH * EXT, LANES), F32)],
    )(tissue, f, rxe, rxo, rye, ryo, w, band)

    adjoint = ((3, 3, DEPTH * OUT, LANES), F32)
    adj, share = call(
        stats_kernel,
        [adjoint, ((8, LANES), F32)],
        [S] + [V] * 7,
        [V] * 2,
        [
            pltpu.VMEM((3, 3, 256, LANES), F32),
            pltpu.VMEM(*adjoint),
            pltpu.VMEM((DEPTH, LANES), F32),
        ],
    )(tissue, rwe, rwo, fx, sums, mask, own, band)

    edge = ((3, GAUSS_RADIUS, DEPTH, 2 * LANES), BF16)
    ys, ge, go = call(
        gradient_kernel,
        [((3, ROWS, DEPTH, 2 * LANES), F32), edge, edge],
        [V] * 7,
        [V] * 3,
        [pltpu.VMEM(*adjoint), pltpu.VMEM((3, 2, ROWS, DEPTH, 3 * LANES), BF16)],
    )(adj, w, fx, slope, band, gh, gl)
    rge, rgo = swap("gx", ge, go)

    nx, ny = lax.axis_size("gx"), lax.axis_size("gy")
    other = lax.ppermute(share, "gy", [(i, i ^ 1) for i in range(ny)])
    line = (share[:1] + other[:1]).reshape(1, 1, LANES)
    groups = [[i * ny + j for i in range(nx) for j in range(p, ny, 2)] for p in range(2)]
    count = nx * ny // 2
    everyone = lax.all_to_all(
        jnp.broadcast_to(line, (count, 1, LANES)), ("gx", "gy"), 0, 0, axis_index_groups=groups
    )
    (loss,) = call(loss_kernel, [((1, LANES), F32)], [V], [V])(everyone.reshape(count, LANES))

    (update,) = call(
        smooth_kernel,
        [((3, rows, 2 * LANES), F32)],
        [V] * 3,
        [A],
        [
            pltpu.VMEM((2, 3, GAUSS_RADIUS, DEPTH, 2 * LANES), F32),
            pltpu.VMEM((rows, LANES), F32),
            pltpu.VMEM((3, 2, rows, LANES), F32),
            pltpu.SemaphoreType.DMA((6,)),
        ],
    )(ys, rge, rgo)
    return update.reshape(velocity.shape), loss[0, 0]


def solution(mesh):
    in_specs = (
        P(None, "gx", "gy"),
        P(None, "gx", "gy"),
        P(None, None, "gx", "gy"),
        P(None, "gx", "gy"),
        P("gx", "gy"),
    )
    out_specs = (P(None, None, "gx", "gy"), P())
    return jax.shard_map(step, mesh=mesh, in_specs=in_specs, out_specs=out_specs, check_vma=False)
```
